32 devices in a mesh: inp: 4 (over y, core), hid: 8 (over z, x).
Axes of the slice: x: 2, y: 2, z: 4, core: 2. Of those that a mesh axis runs over, the one named last changes fastest.
Arguments:
- inputs: bfloat16 [128, 16384], P(None, 'inp'), may hold values from -6 to 6
- out_grad: bfloat16 [128, 16384], P(None, 'inp'), may hold values from -6 to 6
- gate_index: int32 [8192, 26624], P('inp', 'hid'), may hold values from 0 to 255, as said below
- up_index: int32 [8192, 26624], P('inp', 'hid'), may hold values from 0 to 255, as said below
- down_index: int32 [13312, 16384], P('hid', 'inp'), may hold values from 0 to 255, as said below
- gate_table: float32 [16, 26624], P(None, 'hid'), may hold values from -0.046875 to 0.046875
- up_table: float32 [16, 26624], P(None, 'hid'), may hold values from -0.046875 to 0.046875
- down_table: float32 [16, 16384], P(None, 'inp'), may hold values from -0.0390625 to 0.0390625
Outputs:
- input_grad: bfloat16 [128, 16384], P('hid', 'inp')
- gate_table_grad: float32 [16, 26624], P(None, 'hid')
- up_table_grad: float32 [16, 26624], P(None, 'hid')
- down_table_grad: float32 [16, 16384], P(None, 'inp')
The draws below stay inside these ranges and needn't reach their ends.
Inputs may be any that keep to these rules, and one draw needn't show every extreme that they name: `gate_index`: each word holds two independent 4-bit table entries. `up_index`: each word holds two independent 4-bit table entries. `down_index`: each word holds two independent 4-bit table entries.
All inputs are finite; a program needn't handle non-finite values.
Results may differ from the reference program's by a relative error of at most 0.0072.
Values may be sent and summed in bfloat16 or wider, within the bound.
A program may use at most 512 MiB of HBM per device.

```python
import jax
import jax.numpy as jnp
from jax import lax

D = 16384
FF = 26624
ENTRIES = 16
TOKENS = 128
N_HID = 8


def packed_words(key, salt, rows, cols):
    sub = jax.random.fold_in(key, salt)
    words = jax.random.randint(sub, (rows, cols), 0, 256, dtype=jnp.int32)
    return words.at[0, 0].set(255).at[0, 1].set(0)


def draw_gate_index(key, part):
    return packed_words(key, 7101, D // 2, FF)


def draw_up_index(key, part):
    return packed_words(key, 7202, D // 2, FF)


def draw_down_index(key, part):
    return packed_words(key, 7303, FF // 2, D)


def levels(rng, shape, split, low, high):
    def one(dim, blocks):
        steps = jax.random.uniform(jax.random.fold_in(jax.random.fold_in(rng, 6), dim), (blocks,), jnp.float32, low / len(split), high / len(split))
        return jnp.repeat(jnp.exp(steps), shape[dim] // blocks).reshape((-1,) + (1,) * (len(shape) - dim - 1))

    gain = one(*split[0])
    for cut in split[1:]:
        gain = gain * one(*cut)
    return gain


def gaussian(stream_key, extent, scale, most, split=(), held_as=jnp.bfloat16):
    values = jax.random.normal(stream_key, extent, jnp.float32) * scale
    if len(split) > 0:
        values = levels(stream_key, extent, split, -0.22, 0.18) * values
    return jnp.clip(values, min=-most, max=most).astype(held_as)


def setup_inputs(seed: int = 0) -> dict:
    key_of = jax.random.split(jax.random.key(seed), 9)
    inputs = gaussian(key_of[0], (TOKENS, D), 1.0, 6.0, ((1, 4),))
    out_grad = gaussian(key_of[1], (TOKENS, D), 1.0, 6.0, ((1, 4),))
    gate_index = draw_gate_index(jax.random.fold_in(key_of[8], 71), 0)
    up_index = draw_up_index(jax.random.fold_in(key_of[8], 71), 0)
    down_index = draw_down_index(jax.random.fold_in(key_of[8], 71), 0)
    gate_table = gaussian(key_of[5], (ENTRIES, FF), D ** -0.5, 0.046875, ((1, 8),), jnp.float32)
    up_table = gaussian(key_of[6], (ENTRIES, FF), D ** -0.5, 0.046875, ((1, 8),), jnp.float32)
    down_table = gaussian(key_of[7], (ENTRIES, D), FF ** -0.5, 0.0390625, ((1, 4),), jnp.float32)
    return {"inputs": inputs, "out_grad": out_grad, "gate_index": gate_index, "up_index": up_index, "down_index": down_index, "gate_table": gate_table, "up_table": up_table, "down_table": down_table}


def unpack(packed):
    parts = [jnp.bitwise_and(jnp.right_shift(packed, 4 * nibble), 15) for nibble in range(2)]
    stacked = jnp.stack(parts, axis=1)
    return stacked.reshape(packed.shape[0] * 2, packed.shape[1]).astype(jnp.int32)


def decode(indices, lookup):
    summed = jnp.zeros(indices.shape, jnp.float32)
    for bucket in range(16):
        summed = summed + jnp.where(indices == bucket, lookup[bucket][None, :], 0.0)
    return summed.astype(jnp.bfloat16)


def binned(grads, indices):
    return jnp.stack([jnp.sum(jnp.where(indices == bucket, grads, 0.0), axis=0) for bucket in range(16)])


def reference(inputs, out_grad, gate_index, up_index, down_index, gate_table, up_table, down_table):
    blocks = N_HID
    block_width = FF // blocks
    scale = 1.0 / TOKENS

    def one_block(carry, block_id):
        input_acc, down_acc = carry
        begin = (block_id * block_width).astype(jnp.int32)
        packed_begin = (block_id * (block_width // 2)).astype(jnp.int32)
        idx_gate = unpack(lax.dynamic_slice_in_dim(gate_index, begin, block_width, 1))
        idx_up = unpack(lax.dynamic_slice_in_dim(up_index, begin, block_width, 1))
        idx_down = unpack(lax.dynamic_slice_in_dim(down_index, packed_begin, block_width // 2, 0))
        w_gate = decode(idx_gate, lax.dynamic_slice_in_dim(gate_table, begin, block_width, 1))
        w_up = decode(idx_up, lax.dynamic_slice_in_dim(up_table, begin, block_width, 1))
        w_down = decode(idx_down, down_table)
        pre_gate = jnp.dot(inputs, w_gate, preferred_element_type=jnp.float32)
        pre_up = jnp.dot(inputs, w_up, preferred_element_type=jnp.float32)
        hidden_grad = jnp.dot(out_grad, w_down.T, preferred_element_type=jnp.float32)
        sig_gate = jax.nn.sigmoid(pre_gate)
        silu_gate = pre_gate * sig_gate
        activ = (silu_gate * pre_up).astype(jnp.bfloat16)
        gate_grad = (hidden_grad * pre_up * sig_gate * (1.0 + pre_gate * (1.0 - sig_gate))).astype(jnp.bfloat16)
        up_grad = (hidden_grad * silu_gate).astype(jnp.bfloat16)
        input_acc = input_acc + jnp.dot(gate_grad, w_gate.T, preferred_element_type=jnp.float32) + jnp.dot(up_grad, w_up.T, preferred_element_type=jnp.float32)
        gate_bins = binned(jnp.dot(inputs.T, gate_grad, preferred_element_type=jnp.float32), idx_gate) * scale
        up_bins = binned(jnp.dot(inputs.T, up_grad, preferred_element_type=jnp.float32), idx_up) * scale
        down_acc = down_acc + binned(jnp.dot(activ.T, out_grad, preferred_element_type=jnp.float32), idx_down)
        return (input_acc, down_acc), (gate_bins, up_bins)

    start_carry = (jnp.zeros((TOKENS, D), jnp.float32), jnp.zeros((16, D), jnp.float32))
    (input_acc, down_acc), (gate_bins, up_bins) = lax.scan(one_block, start_carry, jnp.arange(blocks, dtype=jnp.int32))
    gate_table_grad = jnp.transpose(gate_bins, (1, 0, 2)).reshape(16, FF)
    up_table_grad = jnp.transpose(up_bins, (1, 0, 2)).reshape(16, FF)
    return input_acc.astype(jnp.bfloat16), gate_table_grad, up_table_grad, down_acc * scale
```

```python
import functools
import math

import jax
import jax.numpy as jnp
from jax import lax
from jax.experimental import pallas as pl
from jax.experimental.pallas import tpu as pltpu
from jax.sharding import PartitionSpec as P

LANES = 128
SUB = 16
ENTRIES = 16
F32 = jnp.float32
BF16 = jnp.bfloat16
LOOKUP = lax.GatherDimensionNumbers(
    offset_dims=(), collapsed_slice_dims=(0,), start_index_map=(0,),
    operand_batching_dims=(1,), start_indices_batching_dims=(1,),
)


def divisor(size, most, unit=LANES):
    best = unit
    for cand in range(unit, most + 1, unit):
        if size % cand == 0:
            best = cand
    return best


def cost(flops, nbytes):
    return pl.CostEstimate(flops=int(flops), bytes_accessed=int(nbytes), transcendentals=0)


def look_up(table, index):
    return lax.gather(
        table, index[..., None], LOOKUP, (1, 1), mode=lax.GatherScatterMode.PROMISE_IN_BOUNDS
    )


def nibbles(words):
    low = jnp.bitwise_and(words.astype(jnp.int16), jnp.int16(15))
    return low, jnp.right_shift(words, 4).astype(jnp.int16)


def lane_chunks(cols):
    return [slice(c * LANES, (c + 1) * LANES) for c in range(cols // LANES)]


def tables_of(table_ref):
    return [table_ref[:, lanes].astype(BF16) for lanes in lane_chunks(table_ref.shape[1])]


def decode_block(idx_ref, tables, i, half):
    columns = []
    for lanes, table in zip(lane_chunks(idx_ref.shape[1]), tables):
        pieces = [[], []]
        for step in range(half // SUB):
            row = pl.multiple_of(i * half + step * SUB, SUB)
            for piece, index in zip(pieces, nibbles(idx_ref[pl.ds(row, SUB), lanes])):
                piece.append(look_up(table, index))
        columns.append(jnp.concatenate(pieces[0] + pieces[1], axis=0))
    return jnp.concatenate(columns, axis=1)


def contract_cols(left, right):
    return lax.dot_general(left, right, (((1,), (1,)), ((), ())), preferred_element_type=F32)


def grouped(count, most, body):
    size = min(count, most)

    def step(j, carry):
        body(j * size, size)
        return carry

    lax.fori_loop(0, count // size, step, 0)
    if count % size:
        body(count - count % size, count % size)


def up_kernel(x_ref, idx_ref, table_ref, pre_ref):
    count, _, block = x_ref.shape
    tables = tables_of(table_ref)
    pre_ref[...] = jnp.zeros_like(pre_ref)

    def body(first, n):
        pre_ref[...] += sum(
            jnp.dot(
                x_ref[first + k], decode_block(idx_ref, tables, first + k, block // 2), preferred_element_type=F32
            )
            for k in range(n)
        )

    grouped(count, 8, body)


def up_product(x_blocks, index, lookup):
    count, tokens, block = x_blocks.shape
    words, width = index.shape
    cols = divisor(width, 256)
    return pl.pallas_call(
        up_kernel,
        grid=(width // cols,),
        in_specs=[
            pl.BlockSpec((count, tokens, block), lambda j: (0, 0, 0)),
            pl.BlockSpec((words, cols), lambda j: (0, j)),
            pl.BlockSpec((ENTRIES, cols), lambda j: (0, j)),
        ],
        out_specs=pl.BlockSpec((tokens, cols), lambda j: (0, j)),
        out_shape=jax.ShapeDtypeStruct((tokens, width), F32),
        cost_estimate=cost(4 * tokens * words * width, 4 * words * width),
        name="up_product",
    )(x_blocks, index, lookup)


def down_kernel(og_ref, idx_ref, table_ref, out_ref):
    count, _, block = out_ref.shape
    tables = tables_of(table_ref)

    @pl.when(pl.program_id(0) == 0)
    def _():
        out_ref[...] = jnp.zeros_like(out_ref)

    def body(first, n):
        for k in range(n):
            out_ref[first + k] += contract_cols(
                og_ref[...], decode_block(idx_ref, tables, first + k, block // 2)
            )

    grouped(count, 3, body)


def down_product(out_grad, index, lookup):
    tokens = out_grad.shape[0]
    words, width = index.shape
    cols = divisor(width, 512)
    block = math.gcd(2 * words, 256)
    count = 2 * words // block
    return pl.pallas_call(
        down_kernel,
        grid=(width // cols,),
        in_specs=[
            pl.BlockSpec((tokens, cols), lambda j: (0, j)),
            pl.BlockSpec((words, cols), lambda j: (0, j)),
            pl.BlockSpec((ENTRIES, cols), lambda j: (0, j)),
        ],
        out_specs=pl.BlockSpec((count, tokens, block), lambda j: (0, 0, 0)),
        out_shape=jax.ShapeDtypeStruct((count, tokens, block), F32),
        cost_estimate=cost(4 * tokens * words * width, 4 * words * width),
        name="down_product",
    )(out_grad, index, lookup)


def signed_sums(sums, value, signs):
    parts = [value]
    for sign in signs:
        parts = parts + [sign * part for part in parts]
    parts = parts[1:]
    return parts if sums is None else [a + b for a, b in zip(sums, parts)]


def write_bins(sums, out_ref, scale):
    step = 1
    while step < ENTRIES:
        mixed = list(sums)
        for k in range(ENTRIES):
            if not k & step:
                mixed[k], mixed[k | step] = sums[k] + sums[k | step], sums[k] - sums[k | step]
        sums = mixed
        step *= 2
    for k in range(ENTRIES):
        out_ref[k : k + 1, :] = sums[k] * (scale / ENTRIES)


def bins_kernel(scale, with_grad, with_start, *refs):
    left_ref, right_ref, total_ref, idx_ref, sign_ref, ones_ref = refs[:6]
    refs = refs[6:]
    if with_grad:
        table_ref, refs = refs[0], refs[1:]
        if with_start:
            start_ref, refs = refs[0], refs[1:]
    out_ref, refs = refs[0], refs[1:]
    if with_grad:
        grad_ref, refs = refs[0], refs[1:]
    acc_ref, values, leaves = refs[0], refs[1:3], refs[3:5]
    count, block, _ = left_ref.shape
    half = block // 2
    cols = idx_ref.shape[1]
    signs = [sign_ref[SUB * b : SUB * b + SUB, :] for b in range(4)]
    if with_grad:
        tables = tables_of(table_ref)

        @pl.when(pl.program_id(0) == 0)
        def _():
            grad_ref[...] = start_ref[...] if with_start else jnp.zeros_like(grad_ref)

    acc_ref[...] = jnp.zeros_like(acc_ref)
    leaves[0][0:SUB, :] = jnp.zeros((SUB, cols), BF16)
    leaves[1][...] = jnp.zeros_like(leaves[1])

    def make(i, slot):
        values[slot][...] = jnp.dot(left_ref[i], right_ref[...], preferred_element_type=F32)

    def grad(i):
        if with_grad:
            grad_ref[i] += contract_cols(right_ref[...], decode_block(idx_ref, tables, i, half))

    def use(i, slot):
        for lanes in lane_chunks(cols):
            sums = None
            for step in range(half // SUB):
                row = pl.multiple_of(i * half + step * SUB, SUB)
                for parity, index in enumerate(nibbles(idx_ref[pl.ds(row, SUB), lanes])):
                    first = parity * half + step * SUB
                    value = values[slot][first : first + SUB, lanes].astype(BF16)
                    sums = signed_sums(sums, value, [look_up(sign, index) for sign in signs])
            for a, total in enumerate(sums):
                leaves[slot][SUB * (a + 1) : SUB * (a + 2), lanes] = total

    def close(slot):
        acc_ref[...] += jnp.dot(ones_ref[...], leaves[slot][...], preferred_element_type=F32)

    make(0, 0)

    def body(j, carry):
        close(1)
        make(2 * j + 1, 1)
        grad(2 * j)
        grad(2 * j + 1)
        use(2 * j, 0)
        close(0)
        make(2 * j + 2, 0)
        use(2 * j + 1, 1)
        return carry

    lax.fori_loop(0, (count - 1) // 2, body, 0)
    close(1)
    last = count - 1
    if count % 2 == 0:
        make(last, 1)
        grad(last - 1)
        grad(last)
        use(last - 1, 0)
        close(0)
        use(last, 1)
        close(1)
    else:
        grad(last)
        use(last, 0)
        close(0)
    whole = jnp.concatenate(
        [
            jnp.sum(right_ref[:, lanes].astype(F32) * total_ref[...], axis=0, keepdims=True)
            for lanes in lane_chunks(cols)
        ],
        axis=1,
    )
    write_bins([whole] + [acc_ref[k : k + 1, :] for k in range(1, ENTRIES)], out_ref, scale)


def sign_table():
    entry = jnp.arange(ENTRIES)[None, :, None]
    bit = jnp.arange(4)[:, None, None]
    sign = 1 - 2 * jnp.bitwise_and(jnp.right_shift(entry, bit), 1)
    return jnp.broadcast_to(sign, (4, ENTRIES, LANES)).reshape(4 * ENTRIES, LANES).astype(BF16)


def group_ones():
    row = jnp.arange(ENTRIES)[:, None]
    col = jnp.arange(ENTRIES * SUB)[None, :]
    return (row == col // SUB).astype(BF16)


def bins(left, total, right, index, scale, lookup=None, start=None):
    count, block, tokens = left.shape
    words, width = index.shape
    cols = divisor(width, 256)
    with_grad, with_start = lookup is not None, start is not None
    whole3 = pl.BlockSpec((count, tokens, block), lambda j: (0, 0, 0))
    in_specs = [
        pl.BlockSpec((count, block, tokens), lambda j: (0, 0, 0)),
        pl.BlockSpec((tokens, cols), lambda j: (0, j)),
        pl.BlockSpec((tokens, LANES), lambda j: (0, 0)),
        pl.BlockSpec((words, cols), lambda j: (0, j)),
        pl.BlockSpec((4 * ENTRIES, LANES), lambda j: (0, 0)),
        pl.BlockSpec((ENTRIES, ENTRIES * SUB), lambda j: (0, 0)),
    ]
    args = [left, right, total, index, sign_table(), group_ones()]
    out_specs = [pl.BlockSpec((ENTRIES, cols), lambda j: (0, j))]
    out_shape = [jax.ShapeDtypeStruct((ENTRIES, width), F32)]
    scratch = [pltpu.VMEM((ENTRIES, cols), F32)]
    scratch += [pltpu.VMEM((block, cols), F32)] * 2 + [pltpu.VMEM((ENTRIES * SUB, cols), BF16)] * 2
    if with_grad:
        in_specs.append(pl.BlockSpec((ENTRIES, cols), lambda j: (0, j)))
        args.append(lookup)
        if with_start:
            in_specs.append(whole3)
            args.append(start)
        out_specs.append(whole3)
        out_shape.append(jax.ShapeDtypeStruct((count, tokens, block), F32))
    out = pl.pallas_call(
        functools.partial(bins_kernel, scale, with_grad, with_start),
        grid=(width // cols,),
        in_specs=in_specs,
        out_specs=out_specs,
        out_shape=out_shape,
        scratch_shapes=scratch,
        cost_estimate=cost(40 * tokens * words * width, 4 * words * width),
        name="bins_grad" if with_grad else "bins",
    )(*args)
    return out if with_grad else out[0]


def row_totals(array):
    total = jnp.sum(array.astype(F32), axis=1, keepdims=True)
    return jnp.broadcast_to(total, (array.shape[0], LANES))


def pairing(block, dtype):
    row = jnp.arange(block)[:, None]
    col = jnp.arange(block)[None, :]
    half = block // 2
    return (row == 2 * (col % half) + col // half).astype(dtype)


def to_blocks(array):
    rows, cols = array.shape
    block = math.gcd(cols, 256)
    out = lax.dot_general(
        array.reshape(rows, cols // block, block), pairing(block, array.dtype), (((2,), (0,)), ((), ())),
        preferred_element_type=F32,
    )
    return jnp.swapaxes(out.astype(array.dtype), 0, 1)


def from_blocks(blocks):
    count, rows, block = blocks.shape
    out = lax.dot_general(
        blocks, pairing(block, blocks.dtype), (((2,), (1,)), ((), ())), precision=lax.Precision.HIGHEST,
        preferred_element_type=F32,
    )
    return jnp.swapaxes(out, 0, 1).reshape(rows, count * block)


def shift(array, axis, size, by):
    return lax.ppermute(array, axis, [(i, i ^ by) for i in range(size)])


def axis_bits(size):
    return [1 << i for i in range(size.bit_length() - 1)]


def power_of_two(size):
    return size & (size - 1) == 0


def sum_scatter(array, axis, dim):
    size = lax.axis_size(axis)
    if not power_of_two(size):
        return lax.psum_scatter(array, axis, scatter_dimension=dim, tiled=True)
    me = lax.axis_index(axis)
    shape = array.shape
    rows = shape[dim] // size
    left = size
    for bit in axis_bits(size):
        left //= 2
        pairs = array.reshape(shape[:dim] + (left, 2, rows) + shape[dim + 1 :])
        mine = jnp.bitwise_and(me // bit, 1)
        sent = lax.dynamic_index_in_dim(pairs, 1 - mine, dim + 1, False).astype(BF16)
        kept = lax.dynamic_index_in_dim(pairs, mine, dim + 1, False)
        array = kept + shift(sent, axis, size, bit).astype(F32)
    return array.reshape(shape[:dim] + (rows,) + shape[dim + 1 :])


def sum_scatter_direct(array, axis, dim):
    size = lax.axis_size(axis)
    if not power_of_two(size):
        return lax.psum_scatter(array, axis, scatter_dimension=dim, tiled=True), []
    me = lax.axis_index(axis)
    rows = array.shape[dim] // size
    total = lax.dynamic_slice_in_dim(array, me * rows, rows, dim)
    sent = [
        shift(
            lax.dynamic_slice_in_dim(array, jnp.bitwise_xor(me, by) * rows, rows, dim).astype(BF16), axis, size, by
        )
        for by in range(1, size)
    ]
    return total, sent


def gather(array, axis):
    size = lax.axis_size(axis)
    if not power_of_two(size):
        return lax.all_gather(array, axis, axis=0, tiled=True)
    me = lax.axis_index(axis)
    rows, cols = array.shape
    array = array[None]
    for bit in reversed(axis_bits(size)):
        other = shift(array, axis, size, bit)
        first = jnp.bitwise_and(me // bit, 1) == 0
        low, high = jnp.where(first, array, other), jnp.where(first, other, array)
        array = jnp.stack([low, high], axis=1).reshape(-1, rows, cols)
    return array.reshape(size * rows, cols)


def sum_all(array, axis):
    size = lax.axis_size(axis)
    if not power_of_two(size):
        return lax.psum(array, axis)
    for bit in axis_bits(size):
        array = array + shift(array, axis, size, bit)
    return array


def after(array, *done):
    return lax.optimization_barrier((array, *done))[0]


def local_hidden(pre_gate, pre_up, hidden_grad):
    sig_gate = jax.nn.sigmoid(pre_gate)
    silu_gate = pre_gate * sig_gate
    activ = (silu_gate * pre_up).astype(BF16)
    gate_grad = (hidden_grad * pre_up * sig_gate * (1.0 + pre_gate * (1.0 - sig_gate))).astype(BF16)
    up_grad = (hidden_grad * silu_gate).astype(BF16)
    return activ, gate_grad, up_grad


def shards(inputs, out_grad, gate_index, up_index, down_index, gate_table, up_table, down_table):
    tokens = inputs.shape[0]
    scale = 1.0 / tokens
    hid_blocks = down_product(out_grad, down_index, down_table)
    hid = sum_scatter(hid_blocks, "inp", 1)
    x_blocks = to_blocks(inputs)
    x_turned = jnp.swapaxes(x_blocks, 1, 2)
    x_total = row_totals(inputs)
    pre_gate = up_product(x_blocks, gate_index, after(gate_table, hid_blocks))
    gate_share = sum_scatter(pre_gate, "inp", 0)
    pre_up = up_product(x_blocks, up_index, after(up_table, pre_gate))
    up_share = sum_scatter(pre_up, "inp", 0)
    activ, gate_grad, up_grad = local_hidden(gate_share, up_share, from_blocks(hid))
    gate_grad = gather(gate_grad, "inp")
    up_grad = gather(after(up_grad, gate_grad), "inp")
    acts = gather(after(activ, gate_grad), "inp")
    gate_part, din_blocks = bins(x_turned, x_total, gate_grad, gate_index, scale, gate_table)
    up_part, din_blocks = bins(
        x_turned, x_total, after(up_grad, gate_part), up_index, scale, up_table, din_blocks
    )
    gate_sum = sum_all(gate_part, "inp")
    din_own, din_sent = sum_scatter_direct(din_blocks, "hid", 1)
    acts = after(acts, up_part)
    down_part = bins(
        jnp.swapaxes(to_blocks(acts), 1, 2), row_totals(acts), out_grad, down_index, scale
    )
    up_sum = sum_all(up_part, "inp")
    down_sum = sum_all(down_part, "hid")
    din = din_own
    for piece in din_sent:
        din = din + after(piece, down_part).astype(F32)
    input_grad = from_blocks(din).astype(BF16)
    return input_grad, gate_sum, up_sum, down_sum


def solution(mesh):
    in_specs = (
        P(None, "inp"),
        P(None, "inp"),
        P("inp", "hid"),
        P("inp", "hid"),
        P("hid", "inp"),
        P(None, "hid"),
        P(None, "hid"),
        P(None, "inp"),
    )
    out_specs = (P("hid", "inp"), P(None, "hid"), P(None, "hid"), P(None, "inp"))
    return jax.shard_map(shards, mesh=mesh, in_specs=in_specs, out_specs=out_specs, check_vma=False)
```

```python
import functools
import math

import jax
import jax.numpy as jnp
from jax import lax
from jax.experimental import pallas as pl
from jax.experimental.pallas import tpu as pltpu
from jax.sharding import PartitionSpec as P

LANES = 128
SUB = 16
ENTRIES = 16
F32 = jnp.float32
BF16 = jnp.bfloat16
LOOKUP = lax.GatherDimensionNumbers(
    offset_dims=(), collapsed_slice_dims=(0,), start_index_map=(0,),
    operand_batching_dims=(1,), start_indices_batching_dims=(1,),
)


def divisor(size, most, unit=LANES):
    best = unit
    for cand in range(unit, most + 1, unit):
        if size % cand == 0:
            best = cand
    return best


def cost(flops, nbytes):
    return pl.CostEstimate(flops=int(flops), bytes_accessed=int(nbytes), transcendentals=0)


def look_up(table, index):
    return lax.gather(
        table, index[..., None], LOOKUP, (1, 1), mode=lax.GatherScatterMode.PROMISE_IN_BOUNDS
    )


def nibbles(words):
    low = jnp.bitwise_and(words.astype(jnp.int16), jnp.int16(15))
    return low, jnp.right_shift(words, 4).astype(jnp.int16)


def lane_chunks(cols):
    return [slice(c * LANES, (c + 1) * LANES) for c in range(cols // LANES)]


def tables_of(table_ref):
    return [table_ref[:, lanes].astype(BF16) for lanes in lane_chunks(table_ref.shape[1])]


def decode_block(idx_ref, tables, i, half):
    columns = []
    for lanes, table in zip(lane_chunks(idx_ref.shape[1]), tables):
        pieces = [[], []]
        for step in range(half // SUB):
            row = pl.multiple_of(i * half + step * SUB, SUB)
            for piece, index in zip(pieces, nibbles(idx_ref[pl.ds(row, SUB), lanes])):
                piece.append(look_up(table, index))
        columns.append(jnp.concatenate(pieces[0] + pieces[1], axis=0))
    return jnp.concatenate(columns, axis=1)


def contract_cols(left, right):
    return lax.dot_general(left, right, (((1,), (1,)), ((), ())), preferred_element_type=F32)


def grouped(count, most, body):
    size = min(count, most)

    def step(j, carry):
        body(j * size, size)
        return carry

    lax.fori_loop(0, count // size, step, 0)
    if count % size:
        body(count - count % size, count % size)


def up_kernel(x_ref, idx_ref, table_ref, pre_ref):
    count, _, block = x_ref.shape
    tables = tables_of(table_ref)
    pre_ref[...] = jnp.zeros_like(pre_ref)

    def body(first, n):
        pre_ref[...] += sum(
            jnp.dot(
                x_ref[first + k], decode_block(idx_ref, tables, first + k, block // 2), preferred_element_type=F32
            )
            for k in range(n)
        )

    grouped(count, 8, body)


def up_product(x_blocks, index, lookup):
    count, tokens, block = x_blocks.shape
    words, width = index.shape
    cols = divisor(width, 256)
    return pl.pallas_call(
        up_kernel,
        grid=(width // cols,),
        in_specs=[
            pl.BlockSpec((count, tokens, block), lambda j: (0, 0, 0)),
            pl.BlockSpec((words, cols), lambda j: (0, j)),
            pl.BlockSpec((ENTRIES, cols), lambda j: (0, j)),
        ],
        out_specs=pl.BlockSpec((tokens, cols), lambda j: (0, j)),
        out_shape=jax.ShapeDtypeStruct((tokens, width), F32),
        cost_estimate=cost(4 * tokens * words * width, 4 * words * width),
        name="up_product",
    )(x_blocks, index, lookup)


def down_kernel(og_ref, idx_ref, table_ref, out_ref):
    count, _, block = out_ref.shape
    tables = tables_of(table_ref)

    @pl.when(pl.program_id(0) == 0)
    def _():
        out_ref[...] = jnp.zeros_like(out_ref)

    def body(first, n):
        for k in range(n):
            out_ref[first + k] += contract_cols(
                og_ref[...], decode_block(idx_ref, tables, first + k, block // 2)
            )

    grouped(count, 3, body)


def down_product(out_grad, index, lookup):
    tokens = out_grad.shape[0]
    words, width = index.shape
    cols = divisor(width, 512)
    block = math.gcd(2 * words, 256)
    count = 2 * words // block
    return pl.pallas_call(
        down_kernel,
        grid=(width // cols,),
        in_specs=[
            pl.BlockSpec((tokens, cols), lambda j: (0, j)),
            pl.BlockSpec((words, cols), lambda j: (0, j)),
            pl.BlockSpec((ENTRIES, cols), lambda j: (0, j)),
        ],
        out_specs=pl.BlockSpec((count, tokens, block), lambda j: (0, 0, 0)),
        out_shape=jax.ShapeDtypeStruct((count, tokens, block), F32),
        cost_estimate=cost(4 * tokens * words * width, 4 * words * width),
        name="down_product",
    )(out_grad, index, lookup)


def signed_sums(sums, value, signs):
    parts = [value]
    for sign in signs:
        parts = parts + [sign * part for part in parts]
    parts = parts[1:]
    return parts if sums is None else [a + b for a, b in zip(sums, parts)]


def bins_tile(left_ref, right_ref, total_ref, idx_ref, sign_ref, ones_ref, acc_ref, values, leaves, grad):
    count, block, _ = left_ref.shape
    half = block // 2
    cols = idx_ref.shape[1]
    signs = [sign_ref[SUB * b : SUB * b + SUB, :] for b in range(4)]
    acc_ref[...] = jnp.zeros_like(acc_ref)
    leaves[0][0:SUB, :] = jnp.zeros((SUB, cols), BF16)
    leaves[1][...] = jnp.zeros_like(leaves[1])

    def make(i, slot):
        values[slot][...] = jnp.dot(left_ref[i], right_ref[...], preferred_element_type=F32)

    def use(i, slot):
        for lanes in lane_chunks(cols):
            runs = []
            sums = None
            for step in range(half // SUB):
                row = pl.multiple_of(i * half + step * SUB, SUB)
                for parity, index in enumerate(nibbles(idx_ref[pl.ds(row, SUB), lanes])):
                    first = parity * half + step * SUB
                    value = values[slot][first : first + SUB, lanes].astype(BF16)
                    sums = signed_sums(sums, value, [look_up(sign, index) for sign in signs])
                if step % 4 == 3 or step == half // SUB - 1:
                    runs.append(sums)
                    sums = None
            while len(runs) > 1:
                runs = [[a + b for a, b in zip(*runs[:2])]] + runs[2:]
            for a, total in enumerate(runs[0]):
                leaves[slot][SUB * (a + 1) : SUB * (a + 2), lanes] = total

    def close(slot):
        acc_ref[...] += jnp.dot(ones_ref[...], leaves[slot][...], preferred_element_type=F32)

    make(0, 0)

    def body(j, carry):
        close(1)
        make(2 * j + 1, 1)
        grad(2 * j)
        grad(2 * j + 1)
        use(2 * j, 0)
        close(0)
        make(jnp.minimum(2 * j + 2, count - 1), 0)
        use(2 * j + 1, 1)
        return carry

    lax.fori_loop(0, count // 2, body, 0)
    close(1)
    if count % 2:
        grad(count - 1)
        use(count - 1, 0)
        close(0)
    whole = jnp.concatenate(
        [
            jnp.sum(right_ref[:, lanes].astype(F32) * total_ref[...], axis=0, keepdims=True)
            for lanes in lane_chunks(cols)
        ],
        axis=1,
    )
    return [whole] + [acc_ref[k : k + 1, :] for k in range(1, ENTRIES)]


def entry_sums(sums):
    step = 1
    while step < ENTRIES:
        mixed = list(sums)
        for k in range(ENTRIES):
            if not k & step:
                mixed[k], mixed[k | step] = sums[k] + sums[k | step], sums[k] - sums[k | step]
        sums = mixed
        step *= 2
    return sums


def grad_kernel(starts, shares, *refs):
    left_ref, right_ref, total_ref, idx_ref, sign_ref, ones_ref, table_ref = refs[:7]
    refs = refs[7:]
    if starts:
        start_ref, refs = refs[0], refs[1:]
    out_ref, sum_ref, acc_ref = refs[:3]
    values, leaves = refs[3:5], refs[5:7]
    grad_ref = refs[7] if shares else sum_ref
    count, _, block = grad_ref.shape
    tables = tables_of(table_ref)

    @pl.when(pl.program_id(0) == 0)
    def _():
        grad_ref[...] = start_ref[...] if starts else jnp.zeros_like(grad_ref)

    def grad(i):
        grad_ref[i] += contract_cols(right_ref[...], decode_block(idx_ref, tables, i, block // 2))

    sums = bins_tile(
        left_ref, right_ref, total_ref, idx_ref, sign_ref, ones_ref, acc_ref, values, leaves, grad
    )
    for k, total in enumerate(entry_sums(sums)):
        out_ref[k : k + 1, :] = total

    if shares:
        rows = sum_ref.shape[2]

        @pl.when(pl.program_id(0) == pl.num_programs(0) - 1)
        def _():
            for p in range(shares):
                sum_ref[p] = grad_ref[:, p * rows : (p + 1) * rows, :].astype(BF16)


def down_bins_kernel(n_hid, n_inp, *refs):
    (left_ref, right_ref, total_ref, idx_ref, sign_ref, ones_ref, gate_ref, up_ref, shares_ref) = refs[:9]
    out_ref, gate_out, up_out, grad_out = refs[9:13]
    acc_ref, values, leaves = refs[13], refs[14:16], refs[16:18]
    (own_ref, got_ref, gate_got, up_got, part_ref, part_got, final_ref) = refs[18:25]
    (own_sem, share_send, share_recv, table_send, table_recv, part_send, part_recv, final_send, final_recv) = refs[25:]
    step, steps = pl.program_id(0), pl.num_programs(0)
    hid, inp = lax.axis_index("hid"), lax.axis_index("inp")
    cols = idx_ref.shape[1]
    rows = ENTRIES // n_hid
    peers = [(k, lax.rem(hid + k, n_hid)) for k in range(1, n_hid)]
    mates = [(k, lax.rem(inp + k, n_inp)) for k in range(1, n_inp)]

    def copies():
        out = []
        for k, peer in peers:
            out.append(pltpu.make_async_remote_copy(
                src_ref=shares_ref.at[peer], dst_ref=got_ref.at[k - 1], send_sem=share_send.at[k - 1],
                recv_sem=share_recv.at[k - 1], device_id={"hid": peer}, device_id_type=pl.DeviceIdType.MESH))
        for k, mate in mates:
            for t, (src, dst) in enumerate(((gate_ref, gate_got), (up_ref, up_got))):
                out.append(pltpu.make_async_remote_copy(
                    src_ref=src, dst_ref=dst.at[k - 1], send_sem=table_send.at[2 * (k - 1) + t],
                    recv_sem=table_recv.at[2 * (k - 1) + t], device_id={"inp": mate},
                    device_id_type=pl.DeviceIdType.MESH))
        return out

    def own_copy():
        return pltpu.make_async_copy(shares_ref.at[hid], own_ref, own_sem)

    def lanes_of(tile):
        return pl.ds(pl.multiple_of(tile * cols, LANES), cols)

    def part_copy(tile, k, peer):
        return pltpu.make_async_remote_copy(
            src_ref=part_ref.at[peer, :, lanes_of(tile)], dst_ref=part_got.at[k - 1, :, lanes_of(tile)],
            send_sem=part_send.at[tile, k - 1], recv_sem=part_recv.at[tile, k - 1], device_id={"hid": peer},
            device_id_type=pl.DeviceIdType.MESH)

    def final_copy(tile, k, peer):
        return pltpu.make_async_remote_copy(
            src_ref=final_ref.at[hid, :, lanes_of(tile)], dst_ref=final_ref.at[hid, :, lanes_of(tile)],
            send_sem=final_send.at[tile, k - 1], recv_sem=final_recv.at[tile, k - 1], device_id={"hid": peer},
            device_id_type=pl.DeviceIdType.MESH)

    @pl.when(step == 0)
    def _():
        barrier = pltpu.get_barrier_semaphore()
        for _, peer in peers:
            pl.semaphore_signal(barrier, inc=1, device_id={"hid": peer}, device_id_type=pl.DeviceIdType.MESH)
        for _, mate in mates:
            pl.semaphore_signal(barrier, inc=1, device_id={"inp": mate}, device_id_type=pl.DeviceIdType.MESH)
        pl.semaphore_wait(barrier, n_hid + n_inp - 2)
        for copy in copies():
            copy.start()
        own_copy().start()

    def settle(tile):
        for k, peer in peers:
            part_copy(tile, k, peer).wait()
        lanes = lanes_of(tile)
        total = part_ref[hid, :, lanes]
        for k, _ in peers:
            total = total + part_got[k - 1, :, lanes]
        final_ref[hid, :, lanes] = total
        for k, peer in peers:
            final_copy(tile, k, peer).start()

    @pl.when(step == steps - 1)
    def _():
        def early(tile, carry):
            settle(tile)
            return carry

        lax.fori_loop(0, steps - 1, early, 0)

    sums = bins_tile(
        left_ref, right_ref, total_ref, idx_ref, sign_ref, ones_ref, acc_ref, values, leaves, lambda i: None
    )
    for k, total in enumerate(entry_sums(sums)):
        part_ref[k // rows, k % rows : k % rows + 1, lanes_of(step)] = total
    for k, peer in peers:
        part_copy(step, k, peer).start()

    @pl.when(step == steps - 1)
    def _():
        for copy in copies():
            copy.wait()
        own_copy().wait()
        for out, own, got in ((gate_out, gate_ref, gate_got), (up_out, up_ref, up_got)):
            total = own[...]
            for k, _ in mates:
                total = total + got[k - 1]
            out[...] = total
        count, _, block = own_ref.shape
        for i in range(count):
            total = own_ref[i].astype(F32)
            for k, _ in peers:
                total = total + got_ref[k - 1, i].astype(F32)
            grad_out[i] = total
        settle(steps - 1)

        def finish(tile, carry):
            for k, peer in peers:
                final_copy(tile, k, peer).wait()
            return carry

        lax.fori_loop(0, steps, finish, 0)
        out_ref[...] = final_ref[...]


def finish_kernel(scale, down_ref, gate_ref, up_ref, grad_ref, order_ref, down_out, gate_out, up_out, grad_out):
    groups, rows, _ = down_ref.shape
    for k in range(groups):
        down_out[k * rows : (k + 1) * rows, :] = down_ref[k] * scale
    gate_out[...] = gate_ref[...] * scale
    up_out[...] = up_ref[...] * scale
    count, _, block = grad_ref.shape
    for i in range(count):
        grad_out[:, i * block : (i + 1) * block] = contract_cols(
            grad_ref[i].astype(BF16), order_ref[...]
        ).astype(BF16)


def finish(down, gate, up, grad, order, scale):
    count, rows, block = grad.shape
    return pl.pallas_call(
        functools.partial(finish_kernel, scale),
        out_shape=[
            jax.ShapeDtypeStruct((ENTRIES, down.shape[2]), F32),
            jax.ShapeDtypeStruct(gate.shape, F32),
            jax.ShapeDtypeStruct(up.shape, F32),
            jax.ShapeDtypeStruct((rows, count * block), BF16),
        ],
        cost_estimate=cost(rows * count * block * block, 8 * gate.size),
        name="finish",
    )(down, gate, up, grad, order)


def sign_table():
    entry = jnp.arange(ENTRIES)[None, :, None]
    bit = jnp.arange(4)[:, None, None]
    sign = 1 - 2 * jnp.bitwise_and(jnp.right_shift(entry, bit), 1)
    return jnp.broadcast_to(sign, (4, ENTRIES, LANES)).reshape(4 * ENTRIES, LANES).astype(BF16)


def group_ones():
    row = jnp.arange(ENTRIES)[:, None]
    col = jnp.arange(ENTRIES * SUB)[None, :]
    return (row == col // SUB).astype(BF16)


def fixed(shape):
    return pl.BlockSpec(shape, lambda j: (0,) * len(shape))


def bins_operands(left, total, right, index, most):
    count, block, tokens = left.shape
    words, width = index.shape
    cols = divisor(width, most)
    specs = [
        fixed((count, block, tokens)),
        pl.BlockSpec((tokens, cols), lambda j: (0, j)),
        fixed((tokens, LANES)),
        pl.BlockSpec((words, cols), lambda j: (0, j)),
        fixed((4 * ENTRIES, LANES)),
        fixed((ENTRIES, ENTRIES * SUB)),
    ]
    scratch = [pltpu.VMEM((ENTRIES, cols), F32)]
    scratch += [pltpu.VMEM((block, cols), F32)] * 2 + [pltpu.VMEM((ENTRIES * SUB, cols), BF16)] * 2
    return cols, specs, [left, right, total, index, sign_table(), group_ones()], scratch


def grad_bins(left, total, right, index, lookup, start=None, shares=0):
    count, block, tokens = left.shape
    words, width = index.shape
    cols, specs, args, scratch = bins_operands(left, total, right, index, 256)
    specs.append(pl.BlockSpec((ENTRIES, cols), lambda j: (0, j)))
    args.append(lookup)
    blocks = (count, tokens, block)
    if start is not None:
        specs.append(fixed(blocks))
        args.append(start)
    if shares:
        grad = jax.ShapeDtypeStruct((shares, count, tokens // shares, block), BF16)
        scratch = scratch + [pltpu.VMEM(blocks, F32)]
    else:
        grad = jax.ShapeDtypeStruct(blocks, F32)
    return pl.pallas_call(
        functools.partial(grad_kernel, start is not None, shares),
        grid=(width // cols,),
        in_specs=specs,
        out_specs=[pl.BlockSpec((ENTRIES, cols), lambda j: (0, j)), fixed(grad.shape)],
        out_shape=[jax.ShapeDtypeStruct((ENTRIES, width), F32), grad],
        scratch_shapes=scratch,
        cost_estimate=cost(40 * tokens * words * width, 4 * words * width),
        name="grad_bins",
    )(*args)


def down_bins(left, total, right, index, gate_part, up_part, shares):
    count, block, tokens = left.shape
    words, width = index.shape
    n_hid, n_inp = lax.axis_size("hid"), lax.axis_size("inp")
    cols, specs, args, scratch = bins_operands(left, total, right, index, 512)
    steps = width // cols
    table = gate_part.shape
    share = shares.shape[1:]
    specs += [fixed(table), fixed(table), pl.BlockSpec(memory_space=pl.ANY)]
    args += [gate_part, up_part, shares]
    rows = ENTRIES // n_hid
    groups = (n_hid, rows, width)
    scratch = scratch + [
        pltpu.VMEM(share, BF16),
        pltpu.VMEM((n_hid - 1,) + share, BF16),
        pltpu.VMEM((n_inp - 1,) + table, F32),
        pltpu.VMEM((n_inp - 1,) + table, F32),
        pltpu.VMEM(groups, F32),
        pltpu.VMEM((n_hid - 1, rows, width), F32),
        pltpu.VMEM(groups, F32),
        pltpu.SemaphoreType.DMA(()),
        pltpu.SemaphoreType.DMA((n_hid - 1,)),
        pltpu.SemaphoreType.DMA((n_hid - 1,)),
        pltpu.SemaphoreType.DMA((2 * (n_inp - 1),)),
        pltpu.SemaphoreType.DMA((2 * (n_inp - 1),)),
        pltpu.SemaphoreType.DMA((steps, n_hid - 1)),
        pltpu.SemaphoreType.DMA((steps, n_hid - 1)),
        pltpu.SemaphoreType.DMA((steps, n_hid - 1)),
        pltpu.SemaphoreType.DMA((steps, n_hid - 1)),
    ]
    return pl.pallas_call(
        functools.partial(down_bins_kernel, n_hid, n_inp),
        grid=(steps,),
        in_specs=specs,
        out_specs=[fixed(groups), fixed(table), fixed(table), fixed(share)],
        out_shape=[
            jax.ShapeDtypeStruct(groups, F32),
            jax.ShapeDtypeStruct(table, F32),
            jax.ShapeDtypeStruct(table, F32),
            jax.ShapeDtypeStruct(share, F32),
        ],
        scratch_shapes=scratch,
        compiler_params=pltpu.CompilerParams(collective_id=0, has_side_effects=True),
        cost_estimate=cost(40 * tokens * words * width, 4 * words * width),
        name="down_bins",
    )(*args)


def row_totals(array):
    total = jnp.sum(array.astype(F32), axis=1, keepdims=True)
    return jnp.broadcast_to(total, (array.shape[0], LANES))


def pairing(block, dtype):
    row = jnp.arange(block)[:, None]
    col = jnp.arange(block)[None, :]
    half = block // 2
    return (row == 2 * (col % half) + col // half).astype(dtype)


def to_blocks(array):
    rows, cols = array.shape
    block = math.gcd(cols, 256)
    out = lax.dot_general(
        array.reshape(rows, cols // block, block), pairing(block, array.dtype), (((2,), (0,)), ((), ())),
        preferred_element_type=F32,
    )
    return jnp.swapaxes(out.astype(array.dtype), 0, 1)


def from_blocks(blocks):
    count, rows, block = blocks.shape
    out = lax.dot_general(
        blocks, pairing(block, blocks.dtype), (((2,), (1,)), ((), ())), precision=lax.Precision.HIGHEST,
        preferred_element_type=F32,
    )
    return jnp.swapaxes(out, 0, 1).reshape(rows, count * block)


def shift(array, axis, size, by):
    return lax.ppermute(array, axis, [(i, i ^ by) for i in range(size)])


def axis_bits(size):
    return [1 << i for i in range(size.bit_length() - 1)]


def power_of_two(size):
    return size & (size - 1) == 0


def sum_scatter(array, axis, dim):
    size = lax.axis_size(axis)
    if not power_of_two(size):
        return lax.psum_scatter(array, axis, scatter_dimension=dim, tiled=True)
    me = lax.axis_index(axis)
    shape = array.shape
    rows = shape[dim] // size
    left = size
    for bit in axis_bits(size):
        left //= 2
        pairs = array.reshape(shape[:dim] + (left, 2, rows) + shape[dim + 1 :])
        mine = jnp.bitwise_and(me // bit, 1)
        sent = lax.dynamic_index_in_dim(pairs, 1 - mine, dim + 1, False).astype(BF16)
        kept = lax.dynamic_index_in_dim(pairs, mine, dim + 1, False)
        array = kept + shift(sent, axis, size, bit).astype(F32)
    return array.reshape(shape[:dim] + (rows,) + shape[dim + 1 :])


def gather(array, axis):
    size = lax.axis_size(axis)
    if not power_of_two(size):
        return lax.all_gather(array, axis, axis=0, tiled=True)
    me = lax.axis_index(axis)
    rows, cols = array.shape
    array = array[None]
    for bit in reversed(axis_bits(size)):
        other = shift(array, axis, size, bit)
        first = jnp.bitwise_and(me // bit, 1) == 0
        low, high = jnp.where(first, array, other), jnp.where(first, other, array)
        array = jnp.stack([low, high], axis=1).reshape(-1, rows, cols)
    return array.reshape(size * rows, cols)


def after(array, *done):
    return lax.optimization_barrier((array, *done))[0]


def local_hidden(pre_gate, pre_up, hidden_grad):
    sig_gate = jax.nn.sigmoid(pre_gate)
    silu_gate = pre_gate * sig_gate
    activ = (silu_gate * pre_up).astype(BF16)
    gate_grad = (hidden_grad * pre_up * sig_gate * (1.0 + pre_gate * (1.0 - sig_gate))).astype(BF16)
    up_grad = (hidden_grad * silu_gate).astype(BF16)
    return activ, gate_grad, up_grad


def shards(inputs, out_grad, gate_index, up_index, down_index, gate_table, up_table, down_table):
    tokens = inputs.shape[0]
    hid_blocks = down_product(out_grad, down_index, down_table)
    hid = sum_scatter(hid_blocks, "inp", 1)
    x_blocks = to_blocks(inputs)
    x_turned = jnp.swapaxes(x_blocks, 1, 2)
    x_total = row_totals(inputs)
    pre_gate = up_product(x_blocks, gate_index, after(gate_table, hid_blocks))
    gate_share = sum_scatter(pre_gate, "inp", 0)
    pre_up = up_product(x_blocks, up_index, after(up_table, pre_gate))
    up_share = sum_scatter(pre_up, "inp", 0)
    activ, gate_grad, up_grad = local_hidden(gate_share, up_share, from_blocks(hid))
    gate_grad = gather(gate_grad, "inp")
    up_grad = gather(after(up_grad, gate_grad), "inp")
    acts = gather(after(activ, gate_grad), "inp")
    gate_part, din_blocks = grad_bins(x_turned, x_total, gate_grad, gate_index, gate_table)
    up_part, shares = grad_bins(
        x_turned, x_total, after(up_grad, gate_part), up_index, up_table, din_blocks, lax.axis_size("hid")
    )
    sums = down_bins(
        jnp.swapaxes(to_blocks(acts), 1, 2), row_totals(acts), out_grad, down_index, gate_part, up_part, shares
    )
    down_sum, gate_sum, up_sum, input_grad = finish(
        *sums, pairing(x_blocks.shape[2], BF16), 1.0 / (tokens * ENTRIES)
    )
    return input_grad, gate_sum, up_sum, down_sum


def solution(mesh):
    in_specs = (
        P(None, "inp"),
        P(None, "inp"),
        P("inp", "hid"),
        P("inp", "hid"),
        P("hid", "inp"),
        P(None, "hid"),
        P(None, "hid"),
        P(None, "inp"),
    )
    out_specs = (P("hid", "inp"), P(None, "hid"), P(None, "hid"), P(None, "inp"))
    return jax.shard_map(shards, mesh=mesh, in_specs=in_specs, out_specs=out_specs, check_vma=False)
```

```python
import functools
import math

import jax
import jax.numpy as jnp
from jax import lax
from jax.experimental import pallas as pl
from jax.experimental.pallas import tpu as pltpu
from jax.sharding import PartitionSpec as P

LANES = 128
SUB = 16
ENTRIES = 16
F32 = jnp.float32
BF16 = jnp.bfloat16
LOOKUP = lax.GatherDimensionNumbers(
    offset_dims=(), collapsed_slice_dims=(0,), start_index_map=(0,),
    operand_batching_dims=(1,), start_indices_batching_dims=(1,),
)


def divisor(size, most, unit=LANES):
    best = unit
    for cand in range(unit, most + 1, unit):
        if size % cand == 0:
            best = cand
    return best


def cost(flops, nbytes):
    return pl.CostEstimate(flops=int(flops), bytes_accessed=int(nbytes), transcendentals=0)


def look_up(table, index):
    return lax.gather(
        table, index[..., None], LOOKUP, (1, 1), mode=lax.GatherScatterMode.PROMISE_IN_BOUNDS
    )


def nibbles(words):
    low = jnp.bitwise_and(words.astype(jnp.int16), jnp.int16(15))
    return low, jnp.right_shift(words, 4).astype(jnp.int16)


def fixed(shape):
    return pl.BlockSpec(shape, lambda j: (0,) * len(shape))


def lane_chunks(cols):
    return [slice(c * LANES, (c + 1) * LANES) for c in range(cols // LANES)]


def tables_of(table_ref):
    return [table_ref[:, lanes].astype(BF16) for lanes in lane_chunks(table_ref.shape[1])]


def decode_block(idx_ref, tables, i, half):
    columns = []
    for lanes, table in zip(lane_chunks(idx_ref.shape[1]), tables):
        pieces = [[], []]
        for step in range(half // SUB):
            row = pl.multiple_of(i * half + step * SUB, SUB)
            for piece, index in zip(pieces, nibbles(idx_ref[pl.ds(row, SUB), lanes])):
                piece.append(look_up(table, index))
        columns.append(jnp.concatenate(pieces[0] + pieces[1], axis=0))
    return jnp.concatenate(columns, axis=1)


def contract_cols(left, right):
    return lax.dot_general(left, right, (((1,), (1,)), ((), ())), preferred_element_type=F32)


def grouped(count, most, body):
    size = min(count, most)

    def step(j, carry):
        body(j * size, size)
        return carry

    lax.fori_loop(0, count // size, step, 0)
    if count % size:
        body(count - count % size, count % size)


LAG_CHIP = 2
LAG_HIDDEN = 5
LAG_RELAY = 8


def mesh_copy(src, dst, send, recv, **device):
    return pltpu.make_async_remote_copy(
        src_ref=src, dst_ref=dst, send_sem=send, recv_sem=recv, device_id=device,
        device_id_type=pl.DeviceIdType.MESH,
    )


def repeat(first, last, body):
    def step(i, carry):
        body(i)
        return carry

    lax.fori_loop(first, last, step, 0)


def hidden_kernel(size, down_steps, *refs):
    (og_ref, x_ref, down_ref, down_table, gate_ref, gate_table, up_ref, up_table, order_ref) = refs[:9]
    (out_ref, hid_acc, hid_part, hid_sib, hid_chip, hid_got, part, sib, chip, chip_got, all_ref) = refs[9:20]
    (hid_send, hid_recv, hid_chip_send, hid_chip_recv, sib_send, sib_recv) = refs[20:26]
    (chip_send, chip_recv, pair_send, pair_recv, far_send, far_recv, relay_send, relay_recv) = refs[26:]
    step, steps = pl.program_id(0), pl.num_programs(0)
    count, _, block = x_ref.shape
    hid_count, tokens, cols = hid_acc.shape
    tiles = hid_count
    chips = size // 2
    rows = tokens // size
    me = lax.axis_index("inp")
    my_chip, side = me // 2, lax.rem(me, 2)
    other = 1 - side
    sibling = 2 * my_chip + other
    far = [(k, lax.rem(my_chip + k, chips)) for k in range(1, chips)]

    def lanes_of(tile):
        return pl.ds(pl.multiple_of(tile * cols, LANES), cols)

    def hid_copy():
        return mesh_copy(hid_part.at[other], hid_sib, hid_send, hid_recv, inp=sibling)

    def hid_far(k, there):
        return mesh_copy(
            hid_chip.at[there], hid_got.at[k - 1], hid_chip_send.at[k - 1], hid_chip_recv.at[k - 1],
            inp=2 * there + side,
        )

    def sib_copy(a, tile):
        lanes = lanes_of(tile)
        return mesh_copy(
            part.at[a, other, :, :, lanes], sib.at[a, :, :, lanes], sib_send.at[a, tile], sib_recv.at[a, tile],
            inp=sibling,
        )

    def chip_copy(a, tile, k, there):
        lanes = lanes_of(tile)
        return mesh_copy(
            chip.at[a, there, :, lanes], chip_got.at[a, k - 1, :, lanes], chip_send.at[a, tile, k - 1],
            chip_recv.at[a, tile, k - 1], inp=2 * there + side,
        )

    def pair_copy(tile):
        own = all_ref.at[me, :, :, lanes_of(tile)]
        return mesh_copy(own, own, pair_send.at[tile], pair_recv.at[tile], inp=sibling)

    def far_copy(tile, k, there):
        own = all_ref.at[me, :, :, lanes_of(tile)]
        return mesh_copy(
            own, own, far_send.at[tile, k - 1], far_recv.at[tile, k - 1], inp=2 * there + side
        )

    def relay_copy(tile, k):
        source = 2 * lax.rem(my_chip + chips - k, chips) + side
        theirs = all_ref.at[source, :, :, lanes_of(tile)]
        return mesh_copy(theirs, theirs, relay_send.at[tile, k - 1], relay_recv.at[tile, k - 1], inp=sibling)

    def hid_sum():
        hid_copy().wait_recv()
        for c in range(chips):
            for i in range(hid_count):
                hid_chip[c, i] = (hid_part[side, c, i].astype(F32) + hid_sib[c, i].astype(F32)).astype(BF16)
        for k, there in far:
            hid_far(k, there).start()

    def chip_sum(u):
        a, tile = u // tiles, lax.rem(u, tiles)
        lanes = lanes_of(tile)
        sib_copy(a, tile).wait_recv()
        for c in range(chips):
            total = part[a, side, c, :, lanes].astype(F32) + sib[a, c, :, lanes].astype(F32)
            chip[a, c, :, lanes] = total.astype(BF16)
        for k, there in far:
            chip_copy(a, tile, k, there).start()

    def hidden(tile):
        lanes = lanes_of(tile)
        shares = []
        for a in range(2):
            total = chip[a, my_chip, :, lanes].astype(F32)
            for k, there in far:
                chip_copy(a, tile, k, there).wait_recv()
                total = total + chip_got[a, k - 1, :, lanes].astype(F32)
            shares.append(total)
        total = hid_chip[my_chip, tile].astype(F32)
        for k, _ in far:
            total = total + hid_got[k - 1, tile].astype(F32)
        high = total.astype(BF16)
        low = (total - high.astype(F32)).astype(BF16)
        grad = contract_cols(high, order_ref[...]) + contract_cols(low, order_ref[...])
        gate_grad, up_grad, activ = local_hidden(shares[0], shares[1], grad)
        all_ref[me, 0, :, lanes] = gate_grad
        all_ref[me, 1, :, lanes] = up_grad
        all_ref[me, 2, :, lanes] = activ
        pair_copy(tile).start()
        for k, there in far:
            far_copy(tile, k, there).start()

    def relay(tile):
        for k, there in far:
            far_copy(tile, k, there).wait_recv()
            relay_copy(tile, k).start()

    @pl.when(step == 0)
    def _():
        barrier = pltpu.get_barrier_semaphore()
        pl.semaphore_signal(barrier, inc=1, device_id={"inp": sibling}, device_id_type=pl.DeviceIdType.MESH)
        for _, there in far:
            pl.semaphore_signal(
                barrier, inc=1, device_id={"inp": 2 * there + side}, device_id_type=pl.DeviceIdType.MESH
            )
        pl.semaphore_wait(barrier, chips)
        hid_acc[...] = jnp.zeros_like(hid_acc)

    @pl.when(step == down_steps + LAG_CHIP)
    def _():
        hid_sum()

    unit = step - down_steps - LAG_CHIP

    @pl.when(unit >= 0)
    def _():
        chip_sum(unit)

    ready = step - down_steps - tiles - LAG_HIDDEN

    @pl.when(ready == 0)
    def _():
        for k, there in far:
            hid_far(k, there).wait_recv()

    @pl.when(ready >= 0)
    def _():
        hidden(ready)

    @pl.when(step >= down_steps + tiles + LAG_RELAY)
    def _():
        relay(step - down_steps - tiles - LAG_RELAY)

    @pl.when(step < down_steps)
    def _():
        tables = tables_of(down_table)

        def body(first, n):
            for k in range(n):
                hid_acc[first + k] += contract_cols(
                    og_ref[...], decode_block(down_ref, tables, first + k, cols // 2)
                )

        grouped(hid_count, 3, body)

    @pl.when(step == down_steps - 1)
    def _():
        for c in range(chips):
            for s in range(2):
                first = (2 * c + s) * rows
                for i in range(hid_count):
                    hid_part[s, c, i] = hid_acc[i, first : first + rows, :].astype(BF16)
        hid_copy().start()

    def product(a, idx_ref, table_ref, tile):
        tables = tables_of(table_ref)
        pre_ref = hid_acc.at[0]
        pre_ref[...] = jnp.zeros_like(pre_ref)

        def body(first, n):
            pre_ref[...] += sum(
                jnp.dot(
                    x_ref[first + k], decode_block(idx_ref, tables, first + k, block // 2),
                    preferred_element_type=F32,
                )
                for k in range(n)
            )

        grouped(count, 8, body)
        for c in range(chips):
            for s in range(2):
                first = (2 * c + s) * rows
                part[a, s, c, :, lanes_of(tile)] = pre_ref[first : first + rows, :].astype(BF16)
        sib_copy(a, tile).start()

    @pl.when(jnp.logical_and(step >= down_steps, step < down_steps + tiles))
    def _():
        product(0, gate_ref, gate_table, step - down_steps)

    @pl.when(step >= down_steps + tiles)
    def _():
        product(1, up_ref, up_table, step - down_steps - tiles)

    @pl.when(step == steps - 1)
    def _():
        repeat(2 * tiles - LAG_CHIP, 2 * tiles, chip_sum)
        repeat(tiles - LAG_HIDDEN, tiles, hidden)
        repeat(tiles - LAG_RELAY, tiles, relay)
        hid_copy().wait_send()
        for k, there in far:
            hid_far(k, there).wait_send()

        def finish_tile(tile):
            for a in range(2):
                sib_copy(a, tile).wait_send()
                for k, there in far:
                    chip_copy(a, tile, k, there).wait_send()
            pair_copy(tile).wait()
            for k, there in far:
                far_copy(tile, k, there).wait_send()
                relay_copy(tile, k).wait()

        repeat(0, tiles, finish_tile)
        out_ref[...] = all_ref[...]


def hidden_grads(x_blocks, out_grad, gate_index, up_index, down_index, gate_table, up_table, down_table, order):
    count, tokens, block = x_blocks.shape
    words, width = gate_index.shape
    down_words, model = down_index.shape
    size = lax.axis_size("inp")
    chips, rows = size // 2, tokens // size
    cols = math.gcd(width, 256)
    tiles = width // cols
    wide = divisor(model, 512)
    down_steps = model // wide
    gathered = (size, 3, rows, width)

    def at(first, last):
        return lambda j: (0, jnp.clip(j - first, 0, last - 1))

    blocks = (tiles, rows, cols)
    dma = pltpu.SemaphoreType.DMA
    return pl.pallas_call(
        functools.partial(hidden_kernel, size, down_steps),
        grid=(down_steps + 2 * tiles,),
        in_specs=[
            pl.BlockSpec((tokens, wide), at(0, down_steps)),
            fixed((count, tokens, block)),
            pl.BlockSpec((down_words, wide), at(0, down_steps)),
            pl.BlockSpec((ENTRIES, wide), at(0, down_steps)),
            pl.BlockSpec((words, cols), at(down_steps, tiles)),
            pl.BlockSpec((ENTRIES, cols), at(down_steps, tiles)),
            pl.BlockSpec((words, cols), at(down_steps + tiles, tiles)),
            pl.BlockSpec((ENTRIES, cols), at(down_steps + tiles, tiles)),
            fixed(order.shape),
        ],
        out_specs=fixed(gathered),
        out_shape=jax.ShapeDtypeStruct(gathered, BF16),
        scratch_shapes=[
            pltpu.VMEM((tiles, tokens, cols), F32),
            pltpu.VMEM((2, chips) + blocks, BF16),
            pltpu.VMEM((chips,) + blocks, BF16),
            pltpu.VMEM((chips,) + blocks, BF16),
            pltpu.VMEM((chips - 1,) + blocks, BF16),
            pltpu.VMEM((2, 2, chips, rows, width), BF16),
            pltpu.VMEM((2, chips, rows, width), BF16),
            pltpu.VMEM((2, chips, rows, width), BF16),
            pltpu.VMEM((2, chips - 1, rows, width), BF16),
            pltpu.VMEM(gathered, BF16),
            dma(()), dma(()), dma((chips - 1,)), dma((chips - 1,)),
            dma((2, tiles)), dma((2, tiles)), dma((2, tiles, chips - 1)), dma((2, tiles, chips - 1)),
            dma((tiles,)), dma((tiles,)), dma((tiles, chips - 1)), dma((tiles, chips - 1)),
            dma((tiles, chips - 1)), dma((tiles, chips - 1)),
        ],
        compiler_params=pltpu.CompilerParams(collective_id=1, has_side_effects=True),
        cost_estimate=cost(12 * tokens * words * width, 12 * words * width),
        name="hidden_grads",
    )(
        out_grad, x_blocks, down_index, down_table, gate_index, gate_table, up_index, up_table, order
    )


def local_hidden(pre_gate, pre_up, hidden_grad):
    sig_gate = jax.nn.sigmoid(pre_gate)
    silu_gate = pre_gate * sig_gate
    activ = (silu_gate * pre_up).astype(BF16)
    gate_grad = (hidden_grad * pre_up * sig_gate * (1.0 + pre_gate * (1.0 - sig_gate))).astype(BF16)
    up_grad = (hidden_grad * silu_gate).astype(BF16)
    return gate_grad, up_grad, activ


def signed_sums(sums, value, signs):
    parts = [value]
    for sign in signs:
        parts = parts + [sign * part for part in parts]
    parts = parts[1:]
    return parts if sums is None else [a + b for a, b in zip(sums, parts)]


def bins_tile(left_ref, right_ref, total_ref, idx_ref, sign_ref, ones_ref, acc_ref, values, leaves, grad):
    count, block, _ = left_ref.shape
    half = block // 2
    cols = idx_ref.shape[1]
    signs = [sign_ref[SUB * b : SUB * b + SUB, :] for b in range(4)]
    acc_ref[...] = jnp.zeros_like(acc_ref)
    leaves[0][0:SUB, :] = jnp.zeros((SUB, cols), BF16)
    leaves[1][...] = jnp.zeros_like(leaves[1])

    def make(i, slot):
        values[slot][...] = jnp.dot(left_ref[i], right_ref[...], preferred_element_type=F32)

    def use(i, slot):
        for lanes in lane_chunks(cols):
            runs = []
            sums = None
            for step in range(half // SUB):
                row = pl.multiple_of(i * half + step * SUB, SUB)
                for parity, index in enumerate(nibbles(idx_ref[pl.ds(row, SUB), lanes])):
                    first = parity * half + step * SUB
                    value = values[slot][first : first + SUB, lanes].astype(BF16)
                    sums = signed_sums(sums, value, [look_up(sign, index) for sign in signs])
                if step % 4 == 3 or step == half // SUB - 1:
                    runs.append(sums)
                    sums = None
            while len(runs) > 1:
                runs = [[a + b for a, b in zip(*runs[:2])]] + runs[2:]
            for a, total in enumerate(runs[0]):
                leaves[slot][SUB * (a + 1) : SUB * (a + 2), lanes] = total

    def close(slot):
        acc_ref[...] += jnp.dot(ones_ref[...], leaves[slot][...], preferred_element_type=F32)

    make(0, 0)

    def body(j, carry):
        close(1)
        make(2 * j + 1, 1)
        grad(2 * j)
        grad(2 * j + 1)
        use(2 * j, 0)
        close(0)
        make(jnp.minimum(2 * j + 2, count - 1), 0)
        use(2 * j + 1, 1)
        return carry

    lax.fori_loop(0, count // 2, body, 0)
    close(1)
    if count % 2:
        grad(count - 1)
        use(count - 1, 0)
        close(0)
    whole = jnp.concatenate(
        [
            jnp.sum(right_ref[:, lanes].astype(F32) * total_ref[...], axis=0, keepdims=True)
            for lanes in lane_chunks(cols)
        ],
        axis=1,
    )
    return [whole] + [acc_ref[k : k + 1, :] for k in range(1, ENTRIES)]


def entry_sums(sums):
    step = 1
    while step < ENTRIES:
        mixed = list(sums)
        for k in range(ENTRIES):
            if not k & step:
                mixed[k], mixed[k | step] = sums[k] + sums[k | step], sums[k] - sums[k | step]
        sums = mixed
        step *= 2
    return sums


def grad_kernel(starts, shares, *refs):
    left_ref, hidden_ref, total_ref, idx_ref, sign_ref, ones_ref, table_ref = refs[:7]
    refs = refs[7:]
    if starts:
        start_ref, refs = refs[0], refs[1:]
    out_ref, sum_ref, right_ref, acc_ref = refs[:4]
    values, leaves = refs[4:6], refs[6:8]
    grad_ref = refs[8] if shares else sum_ref
    size, _, per, _ = hidden_ref.shape
    for p in range(size):
        right_ref[p * per : (p + 1) * per, :] = hidden_ref[p, 0]
    count, _, block = grad_ref.shape
    tables = tables_of(table_ref)

    @pl.when(pl.program_id(0) == 0)
    def _():
        grad_ref[...] = start_ref[...] if starts else jnp.zeros_like(grad_ref)

    def grad(i):
        grad_ref[i] += contract_cols(right_ref[...], decode_block(idx_ref, tables, i, block // 2))

    sums = bins_tile(
        left_ref, right_ref, total_ref, idx_ref, sign_ref, ones_ref, acc_ref, values, leaves, grad
    )
    for k, total in enumerate(entry_sums(sums)):
        out_ref[k : k + 1, :] = total

    if shares:
        rows = sum_ref.shape[2]

        @pl.when(pl.program_id(0) == pl.num_programs(0) - 1)
        def _():
            for p in range(shares):
                sum_ref[p] = grad_ref[:, p * rows : (p + 1) * rows, :].astype(BF16)


def down_bins_kernel(n_hid, n_inp, *refs):
    (left_ref, right_ref, total_ref, idx_ref, sign_ref, ones_ref, gate_ref, up_ref, shares_ref) = refs[:9]
    out_ref, gate_out, up_out, grad_out = refs[9:13]
    acc_ref, values, leaves = refs[13], refs[14:16], refs[16:18]
    (own_ref, got_ref, gate_got, up_got, part_ref, part_got, final_ref) = refs[18:25]
    (own_sem, share_send, share_recv, table_send, table_recv, part_send, part_recv, final_send, final_recv) = refs[25:]
    step, steps = pl.program_id(0), pl.num_programs(0)
    hid, inp = lax.axis_index("hid"), lax.axis_index("inp")
    cols = idx_ref.shape[1]
    rows = ENTRIES // n_hid
    peers = [(k, lax.rem(hid + k, n_hid)) for k in range(1, n_hid)]
    mates = [(k, lax.rem(inp + k, n_inp)) for k in range(1, n_inp)]

    def copies():
        out = []
        for k, peer in peers:
            out.append(pltpu.make_async_remote_copy(
                src_ref=shares_ref.at[peer], dst_ref=got_ref.at[k - 1], send_sem=share_send.at[k - 1],
                recv_sem=share_recv.at[k - 1], device_id={"hid": peer}, device_id_type=pl.DeviceIdType.MESH))
        for k, mate in mates:
            for t, (src, dst) in enumerate(((gate_ref, gate_got), (up_ref, up_got))):
                out.append(pltpu.make_async_remote_copy(
                    src_ref=src, dst_ref=dst.at[k - 1], send_sem=table_send.at[2 * (k - 1) + t],
                    recv_sem=table_recv.at[2 * (k - 1) + t], device_id={"inp": mate},
                    device_id_type=pl.DeviceIdType.MESH))
        return out

    def own_copy():
        return pltpu.make_async_copy(shares_ref.at[hid], own_ref, own_sem)

    def lanes_of(tile):
        return pl.ds(pl.multiple_of(tile * cols, LANES), cols)

    def part_copy(tile, k, peer):
        return pltpu.make_async_remote_copy(
            src_ref=part_ref.at[peer, :, lanes_of(tile)], dst_ref=part_got.at[k - 1, :, lanes_of(tile)],
            send_sem=part_send.at[tile, k - 1], recv_sem=part_recv.at[tile, k - 1], device_id={"hid": peer},
            device_id_type=pl.DeviceIdType.MESH)

    def final_copy(tile, k, peer):
        return pltpu.make_async_remote_copy(
            src_ref=final_ref.at[hid, :, lanes_of(tile)], dst_ref=final_ref.at[hid, :, lanes_of(tile)],
            send_sem=final_send.at[tile, k - 1], recv_sem=final_recv.at[tile, k - 1], device_id={"hid": peer},
            device_id_type=pl.DeviceIdType.MESH)

    @pl.when(step == 0)
    def _():
        barrier = pltpu.get_barrier_semaphore()
        for _, peer in peers:
            pl.semaphore_signal(barrier, inc=1, device_id={"hid": peer}, device_id_type=pl.DeviceIdType.MESH)
        for _, mate in mates:
            pl.semaphore_signal(barrier, inc=1, device_id={"inp": mate}, device_id_type=pl.DeviceIdType.MESH)
        pl.semaphore_wait(barrier, n_hid + n_inp - 2)
        for copy in copies():
            copy.start()
        own_copy().start()

    def settle(tile):
        for k, peer in peers:
            part_copy(tile, k, peer).wait()
        lanes = lanes_of(tile)
        total = part_ref[hid, :, lanes]
        for k, _ in peers:
            total = total + part_got[k - 1, :, lanes]
        final_ref[hid, :, lanes] = total
        for k, peer in peers:
            final_copy(tile, k, peer).start()

    @pl.when(step == steps - 1)
    def _():
        def early(tile, carry):
            settle(tile)
            return carry

        lax.fori_loop(0, steps - 1, early, 0)

    sums = bins_tile(
        left_ref, right_ref, total_ref, idx_ref, sign_ref, ones_ref, acc_ref, values, leaves, lambda i: None
    )
    for k, total in enumerate(entry_sums(sums)):
        part_ref[k // rows, k % rows : k % rows + 1, lanes_of(step)] = total
    for k, peer in peers:
        part_copy(step, k, peer).start()

    @pl.when(step == steps - 1)
    def _():
        for copy in copies():
            copy.wait()
        own_copy().wait()
        for out, own, got in ((gate_out, gate_ref, gate_got), (up_out, up_ref, up_got)):
            total = own[...]
            for k, _ in mates:
                total = total + got[k - 1]
            out[...] = total
        count, _, block = own_ref.shape
        for i in range(count):
            total = own_ref[i].astype(F32)
            for k, _ in peers:
                total = total + got_ref[k - 1, i].astype(F32)
            grad_out[i] = total
        settle(steps - 1)

        def finish(tile, carry):
            for k, peer in peers:
                final_copy(tile, k, peer).wait()
            return carry

        lax.fori_loop(0, steps, finish, 0)
        out_ref[...] = final_ref[...]


def finish_kernel(scale, down_ref, gate_ref, up_ref, grad_ref, order_ref, down_out, gate_out, up_out, grad_out):
    groups, rows, _ = down_ref.shape
    for k in range(groups):
        down_out[k * rows : (k + 1) * rows, :] = down_ref[k] * scale
    gate_out[...] = gate_ref[...] * scale
    up_out[...] = up_ref[...] * scale
    count, _, block = grad_ref.shape
    for i in range(count):
        grad_out[:, i * block : (i + 1) * block] = contract_cols(
            grad_ref[i].astype(BF16), order_ref[...]
        ).astype(BF16)


def finish(down, gate, up, grad, order, scale):
    count, rows, block = grad.shape
    return pl.pallas_call(
        functools.partial(finish_kernel, scale),
        out_shape=[
            jax.ShapeDtypeStruct((ENTRIES, down.shape[2]), F32),
            jax.ShapeDtypeStruct(gate.shape, F32),
            jax.ShapeDtypeStruct(up.shape, F32),
            jax.ShapeDtypeStruct((rows, count * block), BF16),
        ],
        cost_estimate=cost(rows * count * block * block, 8 * gate.size),
        name="finish",
    )(down, gate, up, grad, order)


def sign_table():
    entry = jnp.arange(ENTRIES)[None, :, None]
    bit = jnp.arange(4)[:, None, None]
    sign = 1 - 2 * jnp.bitwise_and(jnp.right_shift(entry, bit), 1)
    return jnp.broadcast_to(sign, (4, ENTRIES, LANES)).reshape(4 * ENTRIES, LANES).astype(BF16)


def group_ones():
    row = jnp.arange(ENTRIES)[:, None]
    col = jnp.arange(ENTRIES * SUB)[None, :]
    return (row == col // SUB).astype(BF16)


def bins_operands(left, total, right, index, most):
    count, block, tokens = left.shape
    words, width = index.shape
    cols = divisor(width, most)
    specs = [
        fixed((count, block, tokens)),
        pl.BlockSpec((tokens, cols), lambda j: (0, j)),
        fixed((tokens, LANES)),
        pl.BlockSpec((words, cols), lambda j: (0, j)),
        fixed((4 * ENTRIES, LANES)),
        fixed((ENTRIES, ENTRIES * SUB)),
    ]
    scratch = [pltpu.VMEM((ENTRIES, cols), F32)]
    scratch += [pltpu.VMEM((block, cols), F32)] * 2 + [pltpu.VMEM((ENTRIES * SUB, cols), BF16)] * 2
    return cols, specs, [left, right, total, index, sign_table(), group_ones()], scratch


def grad_bins(left, total, hidden, which, index, lookup, start=None, shares=0):
    count, block, tokens = left.shape
    words, width = index.shape
    cols, specs, args, scratch = bins_operands(left, total, hidden, index, 256)
    size, _, rows, _ = hidden.shape
    specs[1] = pl.BlockSpec((size, 1, rows, cols), lambda j: (0, which, 0, j))
    scratch = [pltpu.VMEM((tokens, cols), BF16)] + scratch
    specs.append(pl.BlockSpec((ENTRIES, cols), lambda j: (0, j)))
    args.append(lookup)
    blocks = (count, tokens, block)
    if start is not None:
        specs.append(fixed(blocks))
        args.append(start)
    if shares:
        grad = jax.ShapeDtypeStruct((shares, count, tokens // shares, block), BF16)
        scratch = scratch + [pltpu.VMEM(blocks, F32)]
    else:
        grad = jax.ShapeDtypeStruct(blocks, F32)
    return pl.pallas_call(
        functools.partial(grad_kernel, start is not None, shares),
        grid=(width // cols,),
        in_specs=specs,
        out_specs=[pl.BlockSpec((ENTRIES, cols), lambda j: (0, j)), fixed(grad.shape)],
        out_shape=[jax.ShapeDtypeStruct((ENTRIES, width), F32), grad],
        scratch_shapes=scratch,
        cost_estimate=cost(40 * tokens * words * width, 4 * words * width),
        name="grad_bins",
    )(*args)


def down_bins(left, total, right, index, gate_part, up_part, shares):
    count, block, tokens = left.shape
    words, width = index.shape
    n_hid, n_inp = lax.axis_size("hid"), lax.axis_size("inp")
    cols, specs, args, scratch = bins_operands(left, total, right, index, 512)
    steps = width // cols
    table = gate_part.shape
    share = shares.shape[1:]
    specs += [fixed(table), fixed(table), pl.BlockSpec(memory_space=pl.ANY)]
    args += [gate_part, up_part, shares]
    rows = ENTRIES // n_hid
    groups = (n_hid, rows, width)
    scratch = scratch + [
        pltpu.VMEM(share, BF16),
        pltpu.VMEM((n_hid - 1,) + share, BF16),
        pltpu.VMEM((n_inp - 1,) + table, F32),
        pltpu.VMEM((n_inp - 1,) + table, F32),
        pltpu.VMEM(groups, F32),
        pltpu.VMEM((n_hid - 1, rows, width), F32),
        pltpu.VMEM(groups, F32),
        pltpu.SemaphoreType.DMA(()),
        pltpu.SemaphoreType.DMA((n_hid - 1,)),
        pltpu.SemaphoreType.DMA((n_hid - 1,)),
        pltpu.SemaphoreType.DMA((2 * (n_inp - 1),)),
        pltpu.SemaphoreType.DMA((2 * (n_inp - 1),)),
        pltpu.SemaphoreType.DMA((steps, n_hid - 1)),
        pltpu.SemaphoreType.DMA((steps, n_hid - 1)),
        pltpu.SemaphoreType.DMA((steps, n_hid - 1)),
        pltpu.SemaphoreType.DMA((steps, n_hid - 1)),
    ]
    return pl.pallas_call(
        functools.partial(down_bins_kernel, n_hid, n_inp),
        grid=(steps,),
        in_specs=specs,
        out_specs=[fixed(groups), fixed(table), fixed(table), fixed(share)],
        out_shape=[
            jax.ShapeDtypeStruct(groups, F32),
            jax.ShapeDtypeStruct(table, F32),
            jax.ShapeDtypeStruct(table, F32),
            jax.ShapeDtypeStruct(share, F32),
        ],
        scratch_shapes=scratch,
        compiler_params=pltpu.CompilerParams(collective_id=0, has_side_effects=True),
        cost_estimate=cost(40 * tokens * words * width, 4 * words * width),
        name="down_bins",
    )(*args)


def row_totals(array):
    total = jnp.sum(array.astype(F32), axis=1, keepdims=True)
    return jnp.broadcast_to(total, (array.shape[0], LANES))


def pairing(block, dtype):
    row = jnp.arange(block)[:, None]
    col = jnp.arange(block)[None, :]
    half = block // 2
    return (row == 2 * (col % half) + col // half).astype(dtype)


def to_blocks(array):
    rows, cols = array.shape
    block = math.gcd(cols, 256)
    out = lax.dot_general(
        array.reshape(rows, cols // block, block), pairing(block, array.dtype), (((2,), (0,)), ((), ())),
        preferred_element_type=F32,
    )
    return jnp.swapaxes(out.astype(array.dtype), 0, 1)


def shards(inputs, out_grad, gate_index, up_index, down_index, gate_table, up_table, down_table):
    tokens = inputs.shape[0]
    width = gate_index.shape[1]
    x_blocks = to_blocks(inputs)
    order = pairing(x_blocks.shape[2], BF16)
    hidden = hidden_grads(
        x_blocks, out_grad, gate_index, up_index, down_index, gate_table, up_table, down_table,
        pairing(math.gcd(width, 256), BF16),
    )
    x_turned = jnp.swapaxes(x_blocks, 1, 2)
    x_total = row_totals(inputs)
    acts = hidden[:, 2].reshape(tokens, width)
    gate_part, din_blocks = grad_bins(x_turned, x_total, hidden, 0, gate_index, gate_table)
    up_part, shares = grad_bins(
        x_turned, x_total, hidden, 1, up_index, up_table, din_blocks, lax.axis_size("hid")
    )
    sums = down_bins(
        jnp.swapaxes(to_blocks(acts), 1, 2), row_totals(acts), out_grad, down_index, gate_part, up_part, shares
    )
    down_sum, gate_sum, up_sum, input_grad = finish(*sums, order, 1.0 / (tokens * ENTRIES))
    return input_grad, gate_sum, up_sum, down_sum


def solution(mesh):
    in_specs = (
        P(None, "inp"),
        P(None, "inp"),
        P("inp", "hid"),
        P("inp", "hid"),
        P("hid", "inp"),
        P(None, "hid"),
        P(None, "hid"),
        P(None, "inp"),
    )
    out_specs = (P("hid", "inp"), P(None, "hid"), P(None, "hid"), P(None, "inp"))
    return jax.shard_map(shards, mesh=mesh, in_specs=in_specs, out_specs=out_specs, check_vma=False)
```

```python
import functools
import math

import jax
import jax.numpy as jnp
import numpy as np
from jax import lax
from jax.experimental import pallas as pl
from jax.experimental.pallas import tpu as pltpu
from jax.sharding import PartitionSpec as P

LANES = 128
SUB = 16
ENTRIES = 16
F32 = jnp.float32
BF16 = jnp.bfloat16
LOOKUP = lax.GatherDimensionNumbers(
    offset_dims=(), collapsed_slice_dims=(0,), start_index_map=(0,),
    operand_batching_dims=(1,), start_indices_batching_dims=(1,),
)


def divisor(size, most, unit=LANES):
    best = unit
    for cand in range(unit, most + 1, unit):
        if size % cand == 0:
            best = cand
    return best


def cost(flops, nbytes):
    return pl.CostEstimate(flops=int(flops), bytes_accessed=int(nbytes), transcendentals=0)


def look_up(table, index):
    return lax.gather(
        table, index[..., None], LOOKUP, (1, 1), mode=lax.GatherScatterMode.PROMISE_IN_BOUNDS
    )


def nibbles(words):
    words = words.astype(jnp.int16)
    return jnp.bitwise_and(words, jnp.int16(15)), lax.shift_right_logical(words, jnp.int16(4))


def fixed(shape):
    return pl.BlockSpec(shape, lambda j: (0,) * len(shape))


def lane_chunks(cols):
    return [slice(c * LANES, (c + 1) * LANES) for c in range(cols // LANES)]


def tables_of(table_ref):
    return [table_ref[:, lanes].astype(BF16) for lanes in lane_chunks(table_ref.shape[1])]


def decode_block(idx_ref, tables, i, half):
    columns = []
    for lanes, table in zip(lane_chunks(idx_ref.shape[1]), tables):
        pieces = [[], []]
        for step in range(half // SUB):
            row = pl.multiple_of(i * half + step * SUB, SUB)
            for piece, index in zip(pieces, nibbles(idx_ref[pl.ds(row, SUB), lanes])):
                piece.append(look_up(table, index))
        columns.append(jnp.concatenate(pieces[0] + pieces[1], axis=0))
    return jnp.concatenate(columns, axis=1)


def contract_cols(left, right):
    return lax.dot_general(left, right, (((1,), (1,)), ((), ())), preferred_element_type=F32)


def grouped(count, most, body):
    size = min(count, most)

    def step(j, carry):
        body(j * size, size)
        return carry

    lax.fori_loop(0, count // size, step, 0)
    if count % size:
        body(count - count % size, count % size)


LAG_CHIP = 1
LAG_HIDDEN = 3
LAG_RELAY = 5
HIDDEN_FROM = 5
RELAY_FROM = 7


def mesh_copy(src, dst, send, recv, **device):
    return pltpu.make_async_remote_copy(
        src_ref=src, dst_ref=dst, send_sem=send, recv_sem=recv, device_id=device,
        device_id_type=pl.DeviceIdType.MESH,
    )


def repeat(first, last, body):
    def step(i, carry):
        body(i)
        return carry

    lax.fori_loop(first, last, step, 0)


def hidden_kernel(size, down_steps, *refs):
    (og_ref, x_ref, down_ref, down_table, gate_ref, gate_table, up_ref, up_table, order_ref) = refs[:9]
    (out_ref, hid_acc, hid_part, hid_sib, hid_chip, hid_got, part, sib, chip, chip_got, all_ref) = refs[9:20]
    (hid_send, hid_recv, hid_chip_send, hid_chip_recv, sib_send, sib_recv) = refs[20:26]
    (chip_send, chip_recv, pair_send, pair_recv, far_send, far_recv, relay_send, relay_recv) = refs[26:]
    step, steps = pl.program_id(0), pl.num_programs(0)
    count, _, block = x_ref.shape
    hid_count, tokens, cols = hid_acc.shape
    tiles = hid_count
    chips = size // 2
    rows = tokens // size
    me = lax.axis_index("inp")
    my_chip, side = me // 2, lax.rem(me, 2)
    other = 1 - side
    sibling = 2 * my_chip + other
    far = [(k, lax.rem(my_chip + k, chips)) for k in range(1, chips)]

    def lanes_of(tile):
        return pl.ds(pl.multiple_of(tile * cols, LANES), cols)

    def hid_copy():
        return mesh_copy(hid_part.at[other], hid_sib, hid_send, hid_recv, inp=sibling)

    def hid_far(k, there):
        return mesh_copy(
            hid_chip.at[there], hid_got.at[k - 1], hid_chip_send.at[k - 1], hid_chip_recv.at[k - 1],
            inp=2 * there + side,
        )

    def sib_copy(a, tile):
        lanes = lanes_of(tile)
        return mesh_copy(
            part.at[a, other, :, :, lanes], sib.at[a, :, :, lanes], sib_send.at[a, tile], sib_recv.at[a, tile],
            inp=sibling,
        )

    def chip_copy(a, tile, k, there):
        lanes = lanes_of(tile)
        return mesh_copy(
            chip.at[a, there, :, lanes], chip_got.at[a, k - 1, :, lanes], chip_send.at[a, tile, k - 1],
            chip_recv.at[a, tile, k - 1], inp=2 * there + side,
        )

    def pair_copy(tile):
        own = all_ref.at[me, :, :, lanes_of(tile)]
        return mesh_copy(own, own, pair_send.at[tile], pair_recv.at[tile], inp=sibling)

    def far_copy(tile, k, there):
        own = all_ref.at[me, :, :, lanes_of(tile)]
        return mesh_copy(
            own, own, far_send.at[tile, k - 1], far_recv.at[tile, k - 1], inp=2 * there + side
        )

    def relay_copy(tile, k):
        source = 2 * lax.rem(my_chip + chips - k, chips) + side
        theirs = all_ref.at[source, :, :, lanes_of(tile)]
        return mesh_copy(theirs, theirs, relay_send.at[tile, k - 1], relay_recv.at[tile, k - 1], inp=sibling)

    def hid_sum():
        hid_copy().wait_recv()
        for c in range(chips):
            for i in range(hid_count):
                hid_chip[c, i] = (hid_part[side, c, i].astype(F32) + hid_sib[c, i].astype(F32)).astype(BF16)
        for k, there in far:
            hid_far(k, there).start()

    def chip_sum(tile):
        for a in range(2):
            chip_part(a, tile)

    def chip_part(a, tile):
        lanes = lanes_of(tile)
        sib_copy(a, tile).wait_recv()
        for c in range(chips):
            total = part[a, side, c, :, lanes].astype(F32) + sib[a, c, :, lanes].astype(F32)
            chip[a, c, :, lanes] = total.astype(BF16)
        for k, there in far:
            chip_copy(a, tile, k, there).start()

    def hidden(tile):
        lanes = lanes_of(tile)
        shares = []
        for a in range(2):
            total = chip[a, my_chip, :, lanes].astype(F32)
            for k, there in far:
                chip_copy(a, tile, k, there).wait_recv()
                total = total + chip_got[a, k - 1, :, lanes].astype(F32)
            shares.append(total)
        total = hid_chip[my_chip, tile].astype(F32)
        for k, _ in far:
            total = total + hid_got[k - 1, tile].astype(F32)
        high = total.astype(BF16)
        low = (total - high.astype(F32)).astype(BF16)
        grad = contract_cols(high, order_ref[...]) + contract_cols(low, order_ref[...])
        gate_grad, up_grad, activ = local_hidden(shares[0], shares[1], grad)
        all_ref[me, 0, :, lanes] = gate_grad
        all_ref[me, 1, :, lanes] = up_grad
        all_ref[me, 2, :, lanes] = activ
        pair_copy(tile).start()
        for k, there in far:
            far_copy(tile, k, there).start()

    def relay(tile):
        for k, there in far:
            far_copy(tile, k, there).wait_recv()
            relay_copy(tile, k).start()

    @pl.when(step == 0)
    def _():
        barrier = pltpu.get_barrier_semaphore()
        pl.semaphore_signal(barrier, inc=1, device_id={"inp": sibling}, device_id_type=pl.DeviceIdType.MESH)
        for _, there in far:
            pl.semaphore_signal(
                barrier, inc=1, device_id={"inp": 2 * there + side}, device_id_type=pl.DeviceIdType.MESH
            )
        pl.semaphore_wait(barrier, chips)
        hid_acc[...] = jnp.zeros_like(hid_acc)

    unit = step - down_steps - LAG_CHIP

    @pl.when(unit >= 0)
    def _():
        chip_sum(unit)

    turn = step - down_steps

    @pl.when(turn == HIDDEN_FROM)
    def _():
        for k, there in far:
            hid_far(k, there).wait_recv()

    @pl.when(turn >= HIDDEN_FROM)
    def _():
        now = turn - LAG_HIDDEN
        repeat(jnp.where(turn == HIDDEN_FROM, 0, now), now + 1, hidden)

    @pl.when(turn >= RELAY_FROM)
    def _():
        now = turn - LAG_RELAY
        repeat(jnp.where(turn == RELAY_FROM, 0, now), now + 1, relay)

    @pl.when(step < down_steps)
    def _():
        tables = tables_of(down_table)

        def body(first, n):
            for k in range(n):
                hid_acc[first + k] += contract_cols(
                    og_ref[...], decode_block(down_ref, tables, first + k, cols // 2)
                )

        grouped(hid_count, 3, body)

    @pl.when(step == down_steps - 1)
    def _():
        for c in range(chips):
            for s in range(2):
                first = (2 * c + s) * rows
                for i in range(hid_count):
                    hid_part[s, c, i] = hid_acc[i, first : first + rows, :].astype(BF16)
        hid_copy().start()

    def product(tile):
        tables = tables_of(gate_table), tables_of(up_table)
        pre = hid_acc.at[0], hid_acc.at[1]
        for pre_ref in pre:
            pre_ref[...] = jnp.zeros_like(pre_ref)

        def body(first, n):
            for a, idx_ref in enumerate((gate_ref, up_ref)):
                pre[a][...] += sum(
                    jnp.dot(
                        x_ref[first + k], decode_block(idx_ref, tables[a], first + k, block // 2),
                        preferred_element_type=F32,
                    )
                    for k in range(n)
                )

        grouped(count, 8, body)
        for a in range(2):
            for c in range(chips):
                for s in range(2):
                    first = (2 * c + s) * rows
                    part[a, s, c, :, lanes_of(tile)] = pre[a][first : first + rows, :].astype(BF16)
            sib_copy(a, tile).start()

    @pl.when(step >= down_steps)
    def _():
        product(step - down_steps)

    @pl.when(turn == 0)
    def _():
        hid_sum()

    @pl.when(step == steps - 1)
    def _():
        repeat(tiles - LAG_CHIP, tiles, chip_sum)
        repeat(tiles - LAG_HIDDEN, tiles, hidden)
        repeat(tiles - LAG_RELAY, tiles, relay)
        hid_copy().wait_send()
        for k, there in far:
            hid_far(k, there).wait_send()

        def finish_tile(tile):
            for a in range(2):
                sib_copy(a, tile).wait_send()
                for k, there in far:
                    chip_copy(a, tile, k, there).wait_send()
            pair_copy(tile).wait()
            for k, there in far:
                far_copy(tile, k, there).wait_send()
                relay_copy(tile, k).wait()

        repeat(0, tiles, finish_tile)
        out_ref[...] = all_ref[...]


def hidden_grads(x_blocks, out_grad, gate_index, up_index, down_index, gate_table, up_table, down_table, order):
    count, tokens, block = x_blocks.shape
    words, width = gate_index.shape
    down_words, model = down_index.shape
    size = lax.axis_size("inp")
    chips, rows = size // 2, tokens // size
    cols = math.gcd(width, 256)
    tiles = width // cols
    wide = divisor(model, 512)
    down_steps = model // wide
    gathered = (size, 3, rows, width)

    def at(first, last):
        return lambda j: (0, jnp.clip(j - first, 0, last - 1))

    blocks = (tiles, rows, cols)
    dma = pltpu.SemaphoreType.DMA
    return pl.pallas_call(
        functools.partial(hidden_kernel, size, down_steps),
        grid=(down_steps + tiles,),
        in_specs=[
            pl.BlockSpec((tokens, wide), at(0, down_steps)),
            fixed((count, tokens, block)),
            pl.BlockSpec((down_words, wide), at(0, down_steps)),
            pl.BlockSpec((ENTRIES, wide), at(0, down_steps)),
            pl.BlockSpec((words, cols), at(down_steps, tiles)),
            pl.BlockSpec((ENTRIES, cols), at(down_steps, tiles)),
            pl.BlockSpec((words, cols), at(down_steps, tiles)),
            pl.BlockSpec((ENTRIES, cols), at(down_steps, tiles)),
            fixed(order.shape),
        ],
        out_specs=fixed(gathered),
        out_shape=jax.ShapeDtypeStruct(gathered, BF16),
        scratch_shapes=[
            pltpu.VMEM((tiles, tokens, cols), F32),
            pltpu.VMEM((2, chips) + blocks, BF16),
            pltpu.VMEM((chips,) + blocks, BF16),
            pltpu.VMEM((chips,) + blocks, BF16),
            pltpu.VMEM((chips - 1,) + blocks, BF16),
            pltpu.VMEM((2, 2, chips, rows, width), BF16),
            pltpu.VMEM((2, chips, rows, width), BF16),
            pltpu.VMEM((2, chips, rows, width), BF16),
            pltpu.VMEM((2, chips - 1, rows, width), BF16),
            pltpu.VMEM(gathered, BF16),
            dma(()), dma(()), dma((chips - 1,)), dma((chips - 1,)),
            dma((2, tiles)), dma((2, tiles)), dma((2, tiles, chips - 1)), dma((2, tiles, chips - 1)),
            dma((tiles,)), dma((tiles,)), dma((tiles, chips - 1)), dma((tiles, chips - 1)),
            dma((tiles, chips - 1)), dma((tiles, chips - 1)),
        ],
        compiler_params=pltpu.CompilerParams(collective_id=1, has_side_effects=True),
        cost_estimate=cost(12 * tokens * words * width, 12 * words * width),
        name="hidden_grads",
    )(
        out_grad, x_blocks, down_index, down_table, gate_index, gate_table, up_index, up_table, order
    )


def local_hidden(pre_gate, pre_up, hidden_grad):
    sig_gate = jax.nn.sigmoid(pre_gate)
    silu_gate = pre_gate * sig_gate
    activ = (silu_gate * pre_up).astype(BF16)
    gate_grad = (hidden_grad * pre_up * sig_gate * (1.0 + pre_gate * (1.0 - sig_gate))).astype(BF16)
    up_grad = (hidden_grad * silu_gate).astype(BF16)
    return gate_grad, up_grad, activ


def signed_sums(sums, value, signs):
    out = [None] * ENTRIES

    def walk(part, bits, chosen):
        if chosen:
            out[chosen] = part if sums is None else sums[chosen - 1] + part
        for bit in range(bits):
            walk(signs[bit] * part, bit, chosen | 1 << bit)

    walk(value, len(signs), 0)
    return out[1:]


def start_bins(accs, leaf_ref):
    for acc_ref in accs:
        acc_ref[...] = jnp.zeros_like(acc_ref)
    leaf_ref[...] = jnp.zeros_like(leaf_ref)


def make_values(left_ref, right_ref, i, value_ref):
    value_ref[...] = jnp.dot(left_ref[i], right_ref[...], preferred_element_type=F32)


def add_signed(idx_ref, signs, i, value_ref, tables=None):
    half = value_ref.shape[0] // 2
    leaves, weights = [], []
    for c, lanes in enumerate(lane_chunks(idx_ref.shape[1])):
        runs, sums, pieces = [], None, ([], [])
        for step in range(half // SUB):
            row = pl.multiple_of(i * half + step * SUB, SUB)
            for parity, index in enumerate(nibbles(idx_ref[pl.ds(row, SUB), lanes])):
                first = parity * half + step * SUB
                if tables is not None:
                    pieces[parity].append(look_up(tables[c], index))
                value = value_ref[first : first + SUB, lanes].astype(BF16)
                sums = signed_sums(sums, value, [look_up(sign, index) for sign in signs])
            if step % 4 == 3 or step == half // SUB - 1:
                runs.append(sums)
                sums = None
        while len(runs) > 1:
            runs = [[a + b for a, b in zip(*runs[:2])]] + runs[2:]
        leaves.append(runs[0])
        if tables is not None:
            weights.append(jnp.concatenate(pieces[0] + pieces[1], axis=0))
    return leaves, jnp.concatenate(weights, axis=1) if weights else None


def keep_leaves(leaves, leaf_ref):
    for c, sums in enumerate(leaves):
        for a, total in enumerate(sums):
            leaf_ref[SUB * (a + 1) : SUB * (a + 2), c * LANES : (c + 1) * LANES] = total


def close_now(ones_ref, leaves, acc_ref):
    blank = jnp.zeros((SUB, LANES), BF16)
    whole = jnp.concatenate([jnp.concatenate([blank] + sums, axis=0) for sums in leaves], axis=1)
    acc_ref[...] += jnp.dot(ones_ref[...], whole, preferred_element_type=F32)


def close_block(ones_ref, leaf_ref, acc_ref):
    acc_ref[...] += jnp.dot(ones_ref[...], leaf_ref[...], preferred_element_type=F32)


def all_sums(acc_ref, right_ref, total_ref):
    whole = jnp.concatenate(
        [
            jnp.sum(right_ref[:, lanes].astype(F32) * total_ref[...], axis=0, keepdims=True)
            for lanes in lane_chunks(right_ref.shape[1])
        ],
        axis=1,
    )
    return [whole] + [acc_ref[k : k + 1, :] for k in range(1, ENTRIES)]


def signs_of(sign_ref):
    return [sign_ref[SUB * b : SUB * b + SUB, :] for b in range(4)]


def bins_tile(left_ref, right_ref, total_ref, idx_ref, sign_ref, ones_ref, acc_ref, values, leaf_ref):
    count = left_ref.shape[0]
    signs = signs_of(sign_ref)
    start_bins([acc_ref], leaf_ref)
    make_values(left_ref, right_ref, 0, values[0])

    def body(j, carry):
        close_block(ones_ref, leaf_ref, acc_ref)
        make_values(left_ref, right_ref, 2 * j + 1, values[1])
        leaves, _ = add_signed(idx_ref, signs, 2 * j, values[0])
        close_now(ones_ref, leaves, acc_ref)
        make_values(left_ref, right_ref, jnp.minimum(2 * j + 2, count - 1), values[0])
        leaves, _ = add_signed(idx_ref, signs, 2 * j + 1, values[1])
        keep_leaves(leaves, leaf_ref)
        return carry

    lax.fori_loop(0, count // 2, body, 0)
    close_block(ones_ref, leaf_ref, acc_ref)
    if count % 2:
        leaves, _ = add_signed(idx_ref, signs, count - 1, values[0])
        close_now(ones_ref, leaves, acc_ref)
    return all_sums(acc_ref, right_ref, total_ref)


def grad_kernel(
    left_ref, gate_hidden, up_hidden, total_ref, gate_idx, up_idx, sign_ref, ones_ref, gate_table, up_table,
    gate_out, up_out, share_ref, gate_ref, up_ref, gate_acc, up_acc, gate_value, up_value, up_leaf, grad_ref,
):
    count, block, _ = left_ref.shape
    half = block // 2
    size, _, per, _ = gate_hidden.shape
    signs = signs_of(sign_ref)
    tables = tables_of(gate_table), tables_of(up_table)

    @pl.when(pl.program_id(0) == 0)
    def _():
        grad_ref[...] = jnp.zeros_like(grad_ref)

    for p in range(size):
        gate_ref[p * per : (p + 1) * per, :] = gate_hidden[p, 0]
        up_ref[p * per : (p + 1) * per, :] = up_hidden[p, 0]
    start_bins([gate_acc, up_acc], up_leaf)
    make_values(left_ref, gate_ref, 0, gate_value)

    def body(i, carry):
        close_block(ones_ref, up_leaf, up_acc)
        make_values(left_ref, up_ref, i, up_value)
        grad = contract_cols(up_ref[...], decode_block(up_idx, tables[1], i, half))
        leaves, weights = add_signed(gate_idx, signs, i, gate_value, tables[0])
        close_now(ones_ref, leaves, gate_acc)
        grad_ref[i] += grad + contract_cols(gate_ref[...], weights)
        make_values(left_ref, gate_ref, jnp.minimum(i + 1, count - 1), gate_value)
        leaves, _ = add_signed(up_idx, signs, i, up_value)
        keep_leaves(leaves, up_leaf)
        return carry

    lax.fori_loop(0, count, body, 0)
    close_block(ones_ref, up_leaf, up_acc)
    for out, acc_ref, right_ref in ((gate_out, gate_acc, gate_ref), (up_out, up_acc, up_ref)):
        for k, total in enumerate(all_sums(acc_ref, right_ref, total_ref)):
            out[k : k + 1, :] = total

    @pl.when(pl.program_id(0) == pl.num_programs(0) - 1)
    def _():
        shares, _, rows, _ = share_ref.shape
        for p in range(shares):
            share_ref[p] = grad_ref[:, p * rows : (p + 1) * rows, :].astype(BF16)


def down_bins_kernel(n_hid, n_inp, *refs):
    (left_ref, right_ref, total_ref, idx_ref, sign_ref, ones_ref, gate_ref, up_ref, shares_ref) = refs[:9]
    out_ref, gate_out, up_out, grad_out = refs[9:13]
    acc_ref, values, leaf_ref = refs[13], refs[14:16], refs[16]
    (own_ref, got_ref, gate_got, up_got, part_ref, part_got, final_ref) = refs[17:24]
    (own_sem, share_send, share_recv, table_send, table_recv, part_send, part_recv, final_send, final_recv) = refs[24:]
    step, steps = pl.program_id(0), pl.num_programs(0)
    hid, inp = lax.axis_index("hid"), lax.axis_index("inp")
    cols = idx_ref.shape[1]
    rows = ENTRIES // n_hid
    peers = [(k, lax.rem(hid + k, n_hid)) for k in range(1, n_hid)]
    mates = [(k, lax.rem(inp + k, n_inp)) for k in range(1, n_inp)]

    def copies():
        out = []
        for k, peer in peers:
            out.append(pltpu.make_async_remote_copy(
                src_ref=shares_ref.at[peer], dst_ref=got_ref.at[k - 1], send_sem=share_send.at[k - 1],
                recv_sem=share_recv.at[k - 1], device_id={"hid": peer}, device_id_type=pl.DeviceIdType.MESH))
        for k, mate in mates:
            for t, (src, dst) in enumerate(((gate_ref, gate_got), (up_ref, up_got))):
                out.append(pltpu.make_async_remote_copy(
                    src_ref=src, dst_ref=dst.at[k - 1], send_sem=table_send.at[2 * (k - 1) + t],
                    recv_sem=table_recv.at[2 * (k - 1) + t], device_id={"inp": mate},
                    device_id_type=pl.DeviceIdType.MESH))
        return out

    def own_copy():
        return pltpu.make_async_copy(shares_ref.at[hid], own_ref, own_sem)

    def lanes_of(tile):
        return pl.ds(pl.multiple_of(tile * cols, LANES), cols)

    def part_copy(tile, k, peer):
        return pltpu.make_async_remote_copy(
            src_ref=part_ref.at[peer, :, lanes_of(tile)], dst_ref=part_got.at[k - 1, :, lanes_of(tile)],
            send_sem=part_send.at[tile, k - 1], recv_sem=part_recv.at[tile, k - 1], device_id={"hid": peer},
            device_id_type=pl.DeviceIdType.MESH)

    def final_copy(tile, k, peer):
        return pltpu.make_async_remote_copy(
            src_ref=final_ref.at[hid, :, lanes_of(tile)], dst_ref=final_ref.at[hid, :, lanes_of(tile)],
            send_sem=final_send.at[tile, k - 1], recv_sem=final_recv.at[tile, k - 1], device_id={"hid": peer},
            device_id_type=pl.DeviceIdType.MESH)

    @pl.when(step == 0)
    def _():
        barrier = pltpu.get_barrier_semaphore()
        for _, peer in peers:
            pl.semaphore_signal(barrier, inc=1, device_id={"hid": peer}, device_id_type=pl.DeviceIdType.MESH)
        for _, mate in mates:
            pl.semaphore_signal(barrier, inc=1, device_id={"inp": mate}, device_id_type=pl.DeviceIdType.MESH)
        pl.semaphore_wait(barrier, n_hid + n_inp - 2)
        for copy in copies():
            copy.start()
        own_copy().start()

    def settle(tile):
        for k, peer in peers:
            part_copy(tile, k, peer).wait()
        lanes = lanes_of(tile)
        total = part_ref[hid, :, lanes]
        for k, _ in peers:
            total = total + part_got[k - 1, :, lanes]
        final_ref[hid, :, lanes] = total
        for k, peer in peers:
            final_copy(tile, k, peer).start()

    @pl.when(step == steps - 1)
    def _():
        def early(tile, carry):
            settle(tile)
            return carry

        lax.fori_loop(0, steps - 1, early, 0)

    sums = bins_tile(
        left_ref, right_ref, total_ref, idx_ref, sign_ref, ones_ref, acc_ref, values, leaf_ref
    )
    for k, total in enumerate(sums):
        part_ref[k // rows, k % rows : k % rows + 1, lanes_of(step)] = total
    for k, peer in peers:
        part_copy(step, k, peer).start()

    @pl.when(step == steps - 1)
    def _():
        for copy in copies():
            copy.wait()
        own_copy().wait()
        for out, own, got in ((gate_out, gate_ref, gate_got), (up_out, up_ref, up_got)):
            total = own[...]
            for k, _ in mates:
                total = total + got[k - 1]
            out[...] = total
        count, _, block = own_ref.shape
        for i in range(count):
            total = own_ref[i].astype(F32)
            for k, _ in peers:
                total = total + got_ref[k - 1, i].astype(F32)
            grad_out[i] = total
        settle(steps - 1)

        def finish(tile, carry):
            for k, peer in peers:
                final_copy(tile, k, peer).wait()
            return carry

        lax.fori_loop(0, steps, finish, 0)
        out_ref[...] = final_ref[...]


def finish_kernel(
    scale, down_ref, gate_ref, up_ref, grad_ref, order_ref, signs_ref, down_out, gate_out, up_out, grad_out, down_all
):
    groups, rows, _ = down_ref.shape
    for k in range(groups):
        down_all[k * rows : (k + 1) * rows, :] = down_ref[k]
    for sums, out in ((down_all, down_out), (gate_ref, gate_out), (up_ref, up_out)):
        out[...] = scale * jnp.dot(
            signs_ref[...], sums[...], precision=lax.Precision.HIGHEST, preferred_element_type=F32
        )
    count, _, block = grad_ref.shape
    for i in range(count):
        grad_out[:, i * block : (i + 1) * block] = contract_cols(
            grad_ref[i].astype(BF16), order_ref[...]
        ).astype(BF16)


def finish(down, gate, up, grad, order, scale):
    count, rows, block = grad.shape
    return pl.pallas_call(
        functools.partial(finish_kernel, scale),
        out_shape=[
            jax.ShapeDtypeStruct((ENTRIES, down.shape[2]), F32),
            jax.ShapeDtypeStruct(gate.shape, F32),
            jax.ShapeDtypeStruct(up.shape, F32),
            jax.ShapeDtypeStruct((rows, count * block), BF16),
        ],
        scratch_shapes=[pltpu.VMEM((ENTRIES, down.shape[2]), F32)],
        cost_estimate=cost(rows * count * block * block, 8 * gate.size),
        name="finish",
    )(down, gate, up, grad, order, entry_signs())


def entry_signs():
    both = np.arange(ENTRIES)[:, None] & np.arange(ENTRIES)[None, :]
    odd = sum(both >> bit & 1 for bit in range(4)) & 1
    return jnp.asarray(1 - 2 * odd, F32)


def sign_table():
    entry = np.arange(ENTRIES)[None, :, None]
    sign = 1 - 2 * (entry >> np.arange(4)[:, None, None] & 1)
    return jnp.asarray(np.tile(sign, (1, 1, LANES)).reshape(4 * ENTRIES, LANES), BF16)


def group_ones():
    row = np.arange(ENTRIES)[:, None]
    return jnp.asarray(row == np.arange(ENTRIES * SUB)[None, :] // SUB, BF16)


def bins_operands(left, total, right, index, most):
    count, block, tokens = left.shape
    words, width = index.shape
    cols = divisor(width, most)
    specs = [
        fixed((count, block, tokens)),
        pl.BlockSpec((tokens, cols), lambda j: (0, j)),
        fixed((tokens, LANES)),
        pl.BlockSpec((words, cols), lambda j: (0, j)),
        fixed((4 * ENTRIES, LANES)),
        fixed((ENTRIES, ENTRIES * SUB)),
    ]
    scratch = [pltpu.VMEM((ENTRIES, cols), F32)]
    scratch += [pltpu.VMEM((block, cols), F32)] * 2 + [pltpu.VMEM((ENTRIES * SUB, cols), BF16)]
    return cols, specs, [left, right, total, index, sign_table(), group_ones()], scratch


def grad_bins(left, total, hidden, gate_index, up_index, gate_table, up_table, shares):
    count, block, tokens = left.shape
    words, width = gate_index.shape
    size, _, rows, _ = hidden.shape
    cols = divisor(width, 256)
    index = pl.BlockSpec((words, cols), lambda j: (0, j))
    table = pl.BlockSpec((ENTRIES, cols), lambda j: (0, j))
    grad = (shares, count, tokens // shares, block)
    return pl.pallas_call(
        grad_kernel,
        grid=(width // cols,),
        in_specs=[
            fixed((count, block, tokens)),
            pl.BlockSpec((size, 1, rows, cols), lambda j: (0, 0, 0, j)),
            pl.BlockSpec((size, 1, rows, cols), lambda j: (0, 1, 0, j)),
            fixed((tokens, LANES)),
            index,
            index,
            fixed((4 * ENTRIES, LANES)),
            fixed((ENTRIES, ENTRIES * SUB)),
            table,
            table,
        ],
        out_specs=[table, table, fixed(grad)],
        out_shape=[
            jax.ShapeDtypeStruct((ENTRIES, width), F32),
            jax.ShapeDtypeStruct((ENTRIES, width), F32),
            jax.ShapeDtypeStruct(grad, BF16),
        ],
        scratch_shapes=[pltpu.VMEM((tokens, cols), BF16)] * 2
        + [pltpu.VMEM((ENTRIES, cols), F32)] * 2
        + [pltpu.VMEM((block, cols), F32)] * 2
        + [pltpu.VMEM((ENTRIES * SUB, cols), BF16)]
        + [pltpu.VMEM((count, tokens, block), F32)],
        cost_estimate=cost(80 * tokens * words * width, 8 * words * width),
        name="grad_bins",
    )(
        left, hidden, hidden, total, gate_index, up_index, sign_table(), group_ones(), gate_table, up_table
    )


def down_bins(left, total, right, index, gate_part, up_part, shares):
    count, block, tokens = left.shape
    words, width = index.shape
    n_hid, n_inp = lax.axis_size("hid"), lax.axis_size("inp")
    cols, specs, args, scratch = bins_operands(left, total, right, index, 256)
    steps = width // cols
    table = gate_part.shape
    share = shares.shape[1:]
    specs += [fixed(table), fixed(table), pl.BlockSpec(memory_space=pl.ANY)]
    args += [gate_part, up_part, shares]
    rows = ENTRIES // n_hid
    groups = (n_hid, rows, width)
    scratch = scratch + [
        pltpu.VMEM(share, BF16),
        pltpu.VMEM((n_hid - 1,) + share, BF16),
        pltpu.VMEM((n_inp - 1,) + table, F32),
        pltpu.VMEM((n_inp - 1,) + table, F32),
        pltpu.VMEM(groups, F32),
        pltpu.VMEM((n_hid - 1, rows, width), F32),
        pltpu.VMEM(groups, F32),
        pltpu.SemaphoreType.DMA(()),
        pltpu.SemaphoreType.DMA((n_hid - 1,)),
        pltpu.SemaphoreType.DMA((n_hid - 1,)),
        pltpu.SemaphoreType.DMA((2 * (n_inp - 1),)),
        pltpu.SemaphoreType.DMA((2 * (n_inp - 1),)),
        pltpu.SemaphoreType.DMA((steps, n_hid - 1)),
        pltpu.SemaphoreType.DMA((steps, n_hid - 1)),
        pltpu.SemaphoreType.DMA((steps, n_hid - 1)),
        pltpu.SemaphoreType.DMA((steps, n_hid - 1)),
    ]
    return pl.pallas_call(
        functools.partial(down_bins_kernel, n_hid, n_inp),
        grid=(steps,),
        in_specs=specs,
        out_specs=[fixed(groups), fixed(table), fixed(table), fixed(share)],
        out_shape=[
            jax.ShapeDtypeStruct(groups, F32),
            jax.ShapeDtypeStruct(table, F32),
            jax.ShapeDtypeStruct(table, F32),
            jax.ShapeDtypeStruct(share, F32),
        ],
        scratch_shapes=scratch,
        compiler_params=pltpu.CompilerParams(collective_id=0, has_side_effects=True),
        cost_estimate=cost(40 * tokens * words * width, 4 * words * width),
        name="down_bins",
    )(*args)


def row_totals(array):
    total = jnp.sum(array.astype(F32), axis=1, keepdims=True)
    return jnp.broadcast_to(total, (array.shape[0], LANES))


def pairing(block, dtype):
    row = np.arange(block)[:, None]
    col = np.arange(block)[None, :]
    half = block // 2
    return jnp.asarray(row == 2 * (col % half) + col // half, dtype)


def to_blocks(array):
    rows, cols = array.shape
    block = math.gcd(cols, 256)
    out = lax.dot_general(
        array.reshape(rows, cols // block, block), pairing(block, array.dtype), (((2,), (0,)), ((), ())),
        preferred_element_type=F32,
    )
    return jnp.swapaxes(out.astype(array.dtype), 0, 1)


def shards(inputs, out_grad, gate_index, up_index, down_index, gate_table, up_table, down_table):
    tokens = inputs.shape[0]
    width = gate_index.shape[1]
    x_blocks = to_blocks(inputs)
    order = pairing(x_blocks.shape[2], BF16)
    hidden = hidden_grads(
        x_blocks, out_grad, gate_index, up_index, down_index, gate_table, up_table, down_table,
        pairing(math.gcd(width, 256), BF16),
    )
    x_turned = jnp.swapaxes(x_blocks, 1, 2)
    x_total = row_totals(inputs)
    acts = hidden[:, 2].reshape(tokens, width)
    gate_part, up_part, shares = grad_bins(
        x_turned, x_total, hidden, gate_index, up_index, gate_table, up_table, lax.axis_size("hid")
    )
    sums = down_bins(
        jnp.swapaxes(to_blocks(acts), 1, 2), row_totals(acts), out_grad, down_index, gate_part, up_part, shares
    )
    down_sum, gate_sum, up_sum, input_grad = finish(*sums, order, 1.0 / (tokens * ENTRIES))
    return input_grad, gate_sum, up_sum, down_sum


def solution(mesh):
    in_specs = (
        P(None, "inp"),
        P(None, "inp"),
        P("inp", "hid"),
        P("inp", "hid"),
        P("hid", "inp"),
        P(None, "hid"),
        P(None, "hid"),
        P(None, "inp"),
    )
    out_specs = (P("hid", "inp"), P(None, "hid"), P(None, "hid"), P(None, "inp"))
    return jax.shard_map(shards, mesh=mesh, in_specs=in_specs, out_specs=out_specs, check_vma=False)
```

```python
import functools
import math

import jax
import jax.numpy as jnp
import numpy as np
from jax import lax
from jax.experimental import pallas as pl
from jax.experimental.pallas import tpu as pltpu
from jax.sharding import PartitionSpec as P

LANES = 128
SUB = 16
ENTRIES = 16
F32 = jnp.float32
BF16 = jnp.bfloat16
LOOKUP = lax.GatherDimensionNumbers(
    offset_dims=(), collapsed_slice_dims=(0,), start_index_map=(0,),
    operand_batching_dims=(1,), start_indices_batching_dims=(1,),
)


def divisor(size, most, unit=LANES):
    best = unit
    for cand in range(unit, most + 1, unit):
        if size % cand == 0:
            best = cand
    return best


def cost(flops, nbytes):
    return pl.CostEstimate(flops=int(flops), bytes_accessed=int(nbytes), transcendentals=0)


def look_up(table, index):
    return lax.gather(
        table, index[..., None], LOOKUP, (1, 1), mode=lax.GatherScatterMode.PROMISE_IN_BOUNDS
    )


def nibbles(words):
    words = words.astype(jnp.int16)
    return jnp.bitwise_and(words, jnp.int16(15)), lax.shift_right_logical(words, jnp.int16(4))


def fixed(shape):
    return pl.BlockSpec(shape, lambda j: (0,) * len(shape))


def lane_chunks(cols):
    return [slice(c * LANES, (c + 1) * LANES) for c in range(cols // LANES)]


def tables_of(table_ref):
    return [table_ref[:, lanes].astype(BF16) for lanes in lane_chunks(table_ref.shape[1])]


def decode_block(idx_ref, tables, i, half):
    columns = []
    for lanes, table in zip(lane_chunks(idx_ref.shape[1]), tables):
        pieces = [[], []]
        for step in range(half // SUB):
            row = pl.multiple_of(i * half + step * SUB, SUB)
            for piece, index in zip(pieces, nibbles(idx_ref[pl.ds(row, SUB), lanes])):
                piece.append(look_up(table, index))
        columns.append(jnp.concatenate(pieces[0] + pieces[1], axis=0))
    return jnp.concatenate(columns, axis=1)


def contract_cols(left, right):
    return lax.dot_general(left, right, (((1,), (1,)), ((), ())), preferred_element_type=F32)


def grouped(count, most, body):
    size = min(count, most)

    def step(j, carry):
        body(j * size, size)
        return carry

    lax.fori_loop(0, count // size, step, 0)
    if count % size:
        body(count - count % size, count % size)


LATE_TILES = 4
LAG_CHIP = 1
LAG_HIDDEN = 3
LAG_RELAY = 5
HIDDEN_FROM = 5
RELAY_FROM = 7


def mesh_copy(src, dst, send, recv, **device):
    return pltpu.make_async_remote_copy(
        src_ref=src, dst_ref=dst, send_sem=send, recv_sem=recv, device_id=device,
        device_id_type=pl.DeviceIdType.MESH,
    )


def repeat(first, last, body):
    def step(i, carry):
        body(i)
        return carry

    lax.fori_loop(first, last, step, 0)


def hidden_kernel(size, down_steps, *refs):
    (og_ref, x_ref, down_ref, down_table, gate_ref, gate_table, up_ref, up_table, order_ref) = refs[:9]
    (out_ref, hid_acc, hid_part, hid_sib, hid_chip, hid_got, part, sib, chip, chip_got, all_ref) = refs[9:20]
    (hid_send, hid_recv, hid_chip_send, hid_chip_recv, sib_send, sib_recv) = refs[20:26]
    (chip_send, chip_recv, pair_send, pair_recv, far_send, far_recv, relay_send, relay_recv) = refs[26:]
    step, steps = pl.program_id(0), pl.num_programs(0)
    count, _, block = x_ref.shape
    hid_count, tokens, cols = hid_acc.shape
    tiles = hid_count
    chips = size // 2
    rows = tokens // size
    me = lax.axis_index("inp")
    my_chip, side = me // 2, lax.rem(me, 2)
    other = 1 - side
    sibling = 2 * my_chip + other
    far = [(k, lax.rem(my_chip + k, chips)) for k in range(1, chips)]

    def lanes_of(tile):
        return pl.ds(pl.multiple_of(tile * cols, LANES), cols)

    def hid_copy():
        return mesh_copy(hid_part.at[other], hid_sib, hid_send, hid_recv, inp=sibling)

    def hid_far(k, there):
        return mesh_copy(
            hid_chip.at[there], hid_got.at[k - 1], hid_chip_send.at[k - 1], hid_chip_recv.at[k - 1],
            inp=2 * there + side,
        )

    def sib_copy(a, tile):
        lanes = lanes_of(tile)
        return mesh_copy(
            part.at[a, other, :, :, lanes], sib.at[a, :, :, lanes], sib_send.at[a, tile], sib_recv.at[a, tile],
            inp=sibling,
        )

    def chip_copy(a, tile, k, there):
        lanes = lanes_of(tile)
        return mesh_copy(
            chip.at[a, there, :, lanes], chip_got.at[a, k - 1, :, lanes], chip_send.at[a, tile, k - 1],
            chip_recv.at[a, tile, k - 1], inp=2 * there + side,
        )

    def pair_copy(tile):
        own = all_ref.at[me, :, :, lanes_of(tile)]
        return mesh_copy(own, own, pair_send.at[tile], pair_recv.at[tile], inp=sibling)

    def far_copy(tile, k, there):
        own = all_ref.at[me, :, :, lanes_of(tile)]
        return mesh_copy(
            own, own, far_send.at[tile, k - 1], far_recv.at[tile, k - 1], inp=2 * there + side
        )

    def relay_copy(tile, k):
        source = 2 * lax.rem(my_chip + chips - k, chips) + side
        theirs = all_ref.at[source, :, :, lanes_of(tile)]
        return mesh_copy(theirs, theirs, relay_send.at[tile, k - 1], relay_recv.at[tile, k - 1], inp=sibling)

    def hid_sum():
        hid_copy().wait_recv()
        for c in range(chips):
            for i in range(hid_count):
                hid_chip[c, i] = (hid_part[side, c, i].astype(F32) + hid_sib[c, i].astype(F32)).astype(BF16)
        for k, there in far:
            hid_far(k, there).start()

    def chip_sum(tile):
        for a in range(2):
            chip_part(a, tile)

    def chip_part(a, tile):
        lanes = lanes_of(tile)
        sib_copy(a, tile).wait_recv()
        for c in range(chips):
            total = part[a, side, c, :, lanes].astype(F32) + sib[a, c, :, lanes].astype(F32)
            chip[a, c, :, lanes] = total.astype(BF16)
        for k, there in far:
            chip_copy(a, tile, k, there).start()

    def hidden(tile):
        lanes = lanes_of(tile)
        shares = []
        for a in range(2):
            total = chip[a, my_chip, :, lanes].astype(F32)
            for k, there in far:
                chip_copy(a, tile, k, there).wait_recv()
                total = total + chip_got[a, k - 1, :, lanes].astype(F32)
            shares.append(total)
        total = hid_chip[my_chip, tile].astype(F32)
        for k, _ in far:
            total = total + hid_got[k - 1, tile].astype(F32)
        high = total.astype(BF16)
        low = (total - high.astype(F32)).astype(BF16)
        grad = contract_cols(high, order_ref[...]) + contract_cols(low, order_ref[...])
        gate_grad, up_grad, activ = local_hidden(shares[0], shares[1], grad)
        all_ref[me, 0, :, lanes] = gate_grad
        all_ref[me, 1, :, lanes] = up_grad
        all_ref[me, 2, :, lanes] = jnp.dot(activ, order_ref[...], preferred_element_type=F32).astype(BF16)
        pair_copy(tile).start()
        for k, there in far:
            far_copy(tile, k, there).start()

    def relay(tile):
        for k, there in far:
            far_copy(tile, k, there).wait_recv()
            relay_copy(tile, k).start()

    @pl.when(step == 0)
    def _():
        barrier = pltpu.get_barrier_semaphore()
        pl.semaphore_signal(barrier, inc=1, device_id={"inp": sibling}, device_id_type=pl.DeviceIdType.MESH)
        for _, there in far:
            pl.semaphore_signal(
                barrier, inc=1, device_id={"inp": 2 * there + side}, device_id_type=pl.DeviceIdType.MESH
            )
        pl.semaphore_wait(barrier, chips)
        hid_acc[...] = jnp.zeros_like(hid_acc)

    unit = step - down_steps - LAG_CHIP

    @pl.when(unit >= 0)
    def _():
        chip_sum(unit)

    turn = step - down_steps

    @pl.when(turn == HIDDEN_FROM)
    def _():
        for k, there in far:
            hid_far(k, there).wait_recv()

    @pl.when(turn >= HIDDEN_FROM)
    def _():
        now = turn - LAG_HIDDEN
        repeat(jnp.where(turn == HIDDEN_FROM, 0, now), now + 1, hidden)

    @pl.when(turn >= RELAY_FROM)
    def _():
        now = turn - LAG_RELAY
        repeat(jnp.where(turn == RELAY_FROM, 0, now), now + 1, relay)

    @pl.when(step < down_steps)
    def _():
        tables = tables_of(down_table)

        def body(first, n):
            for k in range(n):
                hid_acc[first + k] += contract_cols(
                    og_ref[...], decode_block(down_ref, tables, first + k, cols // 2)
                )

        grouped(hid_count, 7, body)

    @pl.when(step == down_steps - 1)
    def _():
        for c in range(chips):
            for s in range(2):
                first = (2 * c + s) * rows
                for i in range(hid_count):
                    hid_part[s, c, i] = hid_acc[i, first : first + rows, :].astype(BF16)
        hid_copy().start()

    def product(tile):
        tables = tables_of(gate_table), tables_of(up_table)
        pre = hid_acc.at[0], hid_acc.at[1]
        for pre_ref in pre:
            pre_ref[...] = jnp.zeros_like(pre_ref)

        def body(first, n):
            for a, idx_ref in enumerate((gate_ref, up_ref)):
                pre[a][...] += sum(
                    jnp.dot(
                        x_ref[first + k], decode_block(idx_ref, tables[a], first + k, block // 2),
                        preferred_element_type=F32,
                    )
                    for k in range(n)
                )

        grouped(count, 16, body)
        for a in range(2):
            for c in range(chips):
                for s in range(2):
                    first = (2 * c + s) * rows
                    part[a, s, c, :, lanes_of(tile)] = pre[a][first : first + rows, :].astype(BF16)
            sib_copy(a, tile).start()

    @pl.when(step >= down_steps)
    def _():
        product(step - down_steps)

    @pl.when(turn == 0)
    def _():
        hid_sum()

    @pl.when(step == steps - 1)
    def _():
        repeat(tiles - LAG_CHIP, tiles, chip_sum)
        repeat(tiles - LAG_HIDDEN, tiles, hidden)
        repeat(tiles - LAG_RELAY, tiles, relay)
        hid_copy().wait_send()
        for k, there in far:
            hid_far(k, there).wait_send()

        def finish_tile(tile):
            for a in range(2):
                sib_copy(a, tile).wait_send()
                for k, there in far:
                    chip_copy(a, tile, k, there).wait_send()
            pair_copy(tile).wait()
            for k, there in far:
                far_copy(tile, k, there).wait_send()
                relay_copy(tile, k).wait()

        repeat(0, tiles, finish_tile)
        out_ref[...] = all_ref[...]


def hidden_grads(x_blocks, out_grad, gate_index, up_index, down_index, gate_table, up_table, down_table, order):
    count, tokens, block = x_blocks.shape
    words, width = gate_index.shape
    down_words, model = down_index.shape
    size = lax.axis_size("inp")
    chips, rows = size // 2, tokens // size
    cols = math.gcd(width, 256)
    tiles = width // cols
    wide = divisor(model, 512)
    down_steps = model // wide
    gathered = (size, 3, rows, width)

    def at(first, last):
        return lambda j: (0, jnp.clip(j - first, 0, last - 1))

    blocks = (tiles, rows, cols)
    dma = pltpu.SemaphoreType.DMA
    return pl.pallas_call(
        functools.partial(hidden_kernel, size, down_steps),
        grid=(down_steps + tiles,),
        in_specs=[
            pl.BlockSpec((tokens, wide), at(0, down_steps)),
            fixed((count, tokens, block)),
            pl.BlockSpec((down_words, wide), at(0, down_steps)),
            pl.BlockSpec((ENTRIES, wide), at(0, down_steps)),
            pl.BlockSpec((words, cols), at(down_steps, tiles)),
            pl.BlockSpec((ENTRIES, cols), at(down_steps, tiles)),
            pl.BlockSpec((words, cols), at(down_steps, tiles)),
            pl.BlockSpec((ENTRIES, cols), at(down_steps, tiles)),
            fixed(order.shape),
        ],
        out_specs=fixed(gathered),
        out_shape=jax.ShapeDtypeStruct(gathered, BF16),
        scratch_shapes=[
            pltpu.VMEM((tiles, tokens, cols), F32),
            pltpu.VMEM((2, chips) + blocks, BF16),
            pltpu.VMEM((chips,) + blocks, BF16),
            pltpu.VMEM((chips,) + blocks, BF16),
            pltpu.VMEM((chips - 1,) + blocks, BF16),
            pltpu.VMEM((2, 2, chips, rows, width), BF16),
            pltpu.VMEM((2, chips, rows, width), BF16),
            pltpu.VMEM((2, chips, rows, width), BF16),
            pltpu.VMEM((2, chips - 1, rows, width), BF16),
            pltpu.VMEM(gathered, BF16),
            dma(()), dma(()), dma((chips - 1,)), dma((chips - 1,)),
            dma((2, tiles)), dma((2, tiles)), dma((2, tiles, chips - 1)), dma((2, tiles, chips - 1)),
            dma((tiles,)), dma((tiles,)), dma((tiles, chips - 1)), dma((tiles, chips - 1)),
            dma((tiles, chips - 1)), dma((tiles, chips - 1)),
        ],
        compiler_params=pltpu.CompilerParams(collective_id=1, has_side_effects=True),
        cost_estimate=cost(12 * tokens * words * width, 12 * words * width),
        name="hidden_grads",
    )(
        out_grad, x_blocks, down_index, down_table, gate_index, gate_table, up_index, up_table, order
    )


def local_hidden(pre_gate, pre_up, hidden_grad):
    sig_gate = jax.nn.sigmoid(pre_gate)
    silu_gate = pre_gate * sig_gate
    activ = (silu_gate * pre_up).astype(BF16)
    gate_grad = (hidden_grad * pre_up * sig_gate * (1.0 + pre_gate * (1.0 - sig_gate))).astype(BF16)
    up_grad = (hidden_grad * silu_gate).astype(BF16)
    return gate_grad, up_grad, activ


def signed_sums(sums, value, signs):
    out = [None] * ENTRIES

    def walk(part, bits, chosen):
        if chosen:
            out[chosen] = part if sums is None else sums[chosen - 1] + part
        for bit in range(bits):
            walk(signs[bit] * part, bit, chosen | 1 << bit)

    walk(value, len(signs), 0)
    return out[1:]


def start_bins(accs, leaf_ref):
    for acc_ref in accs:
        acc_ref[...] = jnp.zeros_like(acc_ref)
    leaf_ref[...] = jnp.zeros_like(leaf_ref)


def make_values(left_ref, right_ref, i, value_ref):
    value_ref[...] = jnp.dot(left_ref[i], right_ref[...], preferred_element_type=F32)


def add_signed(idx_ref, signs, i, value_ref, tables=None):
    half = value_ref.shape[0] // 2
    leaves, weights = [], []
    for c, lanes in enumerate(lane_chunks(idx_ref.shape[1])):
        runs, sums, pieces = [], None, ([], [])
        for step in range(half // SUB):
            row = pl.multiple_of(i * half + step * SUB, SUB)
            for parity, index in enumerate(nibbles(idx_ref[pl.ds(row, SUB), lanes])):
                first = parity * half + step * SUB
                if tables is not None:
                    pieces[parity].append(look_up(tables[c], index))
                value = value_ref[first : first + SUB, lanes].astype(BF16)
                sums = signed_sums(sums, value, [look_up(sign, index) for sign in signs])
            if step % 4 == 3 or step == half // SUB - 1:
                runs.append(sums)
                sums = None
        while len(runs) > 1:
            runs = [[a + b for a, b in zip(*runs[:2])]] + runs[2:]
        leaves.append(runs[0])
        if tables is not None:
            weights.append(jnp.concatenate(pieces[0] + pieces[1], axis=0))
    return leaves, jnp.concatenate(weights, axis=1) if weights else None


def keep_leaves(leaves, leaf_ref):
    for c, sums in enumerate(leaves):
        for a, total in enumerate(sums):
            leaf_ref[SUB * (a + 1) : SUB * (a + 2), c * LANES : (c + 1) * LANES] = total


def close_now(ones_ref, leaves, acc_ref):
    blank = jnp.zeros((SUB, LANES), BF16)
    whole = jnp.concatenate([jnp.concatenate([blank] + sums, axis=0) for sums in leaves], axis=1)
    acc_ref[...] += jnp.dot(ones_ref[...], whole, preferred_element_type=F32)


def close_block(ones_ref, leaf_ref, acc_ref):
    acc_ref[...] += jnp.dot(ones_ref[...], leaf_ref[...], preferred_element_type=F32)


def take_totals(left_ref, total_ref):
    count, block, tokens = left_ref.shape
    totals = [jnp.zeros((8, tokens), F32)] * 8
    for i in range(count):
        for first in range(0, block, SUB):
            rows = left_ref[i, first : first + SUB, :].astype(F32)
            k = first // SUB % 4 * 2
            totals[k : k + 2] = totals[k] + rows[:8], totals[k + 1] + rows[8:]
    total = sum(totals)
    rest = jnp.broadcast_to(jnp.sum(total, axis=0, keepdims=True), total_ref.shape)
    row = lax.broadcasted_iota(jnp.int32, total_ref.shape, 0)
    parts = jnp.zeros(total_ref.shape, F32)
    for k in range(3):
        part = rest.astype(BF16).astype(F32)
        parts = jnp.where(row == k, part, parts)
        rest = rest - part
    total_ref[...] = parts.astype(BF16)


def empty_sum(right_ref, total_ref):
    whole = jnp.dot(total_ref[...], right_ref[...], preferred_element_type=F32)
    return whole[:1] + whole[1:2] + whole[2:3]


def signs_of(sign_ref):
    return [sign_ref[SUB * b : SUB * b + SUB, :] for b in range(4)]


def bins_tile(left_ref, right_ref, idx_ref, sign_ref, ones_ref, acc_ref, values, leaf_ref):
    count = left_ref.shape[0]
    signs = signs_of(sign_ref)
    start_bins([acc_ref], leaf_ref)
    make_values(left_ref, right_ref, 0, values[0])

    def body(j, carry):
        close_block(ones_ref, leaf_ref, acc_ref)
        make_values(left_ref, right_ref, 2 * j + 1, values[1])
        leaves, _ = add_signed(idx_ref, signs, 2 * j, values[0])
        close_now(ones_ref, leaves, acc_ref)
        make_values(left_ref, right_ref, jnp.minimum(2 * j + 2, count - 1), values[0])
        leaves, _ = add_signed(idx_ref, signs, 2 * j + 1, values[1])
        keep_leaves(leaves, leaf_ref)
        return carry

    lax.fori_loop(0, count // 2, body, 0)
    close_block(ones_ref, leaf_ref, acc_ref)
    if count % 2:
        leaves, _ = add_signed(idx_ref, signs, count - 1, values[0])
        close_now(ones_ref, leaves, acc_ref)


def grad_kernel(
    left_ref, gate_hidden, up_hidden, gate_idx, up_idx, sign_ref, ones_ref, gate_table, up_table,
    gate_out, up_out, share_ref, gate_ref, up_ref, gate_acc, up_acc, gate_value, up_value, up_leaf, grad_ref,
    total_ref,
):
    count, block, _ = left_ref.shape
    half = block // 2
    size, _, per, _ = gate_hidden.shape
    signs = signs_of(sign_ref)
    tables = tables_of(gate_table), tables_of(up_table)

    @pl.when(pl.program_id(0) == 0)
    def _():
        grad_ref[...] = jnp.zeros_like(grad_ref)
        take_totals(left_ref, total_ref)

    for p in range(size):
        gate_ref[p * per : (p + 1) * per, :] = gate_hidden[p, 0]
        up_ref[p * per : (p + 1) * per, :] = up_hidden[p, 0]
    gate_out[0:1, :] = empty_sum(gate_ref, total_ref)
    up_out[0:1, :] = empty_sum(up_ref, total_ref)
    start_bins([gate_acc, up_acc], up_leaf)
    make_values(left_ref, gate_ref, 0, gate_value)

    def body(i, carry):
        close_block(ones_ref, up_leaf, up_acc)
        make_values(left_ref, up_ref, i, up_value)
        grad = contract_cols(up_ref[...], decode_block(up_idx, tables[1], i, half))
        leaves, weights = add_signed(gate_idx, signs, i, gate_value, tables[0])
        close_now(ones_ref, leaves, gate_acc)
        grad_ref[i] += grad + contract_cols(gate_ref[...], weights)
        make_values(left_ref, gate_ref, jnp.minimum(i + 1, count - 1), gate_value)
        leaves, _ = add_signed(up_idx, signs, i, up_value)
        keep_leaves(leaves, up_leaf)
        return carry

    lax.fori_loop(0, count, body, 0)
    close_block(ones_ref, up_leaf, up_acc)
    for out, acc_ref in ((gate_out, gate_acc), (up_out, up_acc)):
        out[1:, :] = acc_ref[1:, :]

    @pl.when(pl.program_id(0) == pl.num_programs(0) - 1)
    def _():
        shares, _, rows, _ = share_ref.shape
        for p in range(shares):
            share_ref[p] = grad_ref[:, p * rows : (p + 1) * rows, :].astype(BF16)


def down_bins_kernel(n_hid, n_inp, tiles, *refs):
    (left_ref, right_ref, idx_ref, sign_ref, ones_ref, gate_ref, up_ref, shares_ref) = refs[:8]
    out_ref, gate_out, up_out, grad_out = refs[8:12]
    total_ref, acc_ref, values, leaf_ref = refs[12], refs[13], refs[14:16], refs[16]
    (own_ref, got_ref, gate_got, up_got, part_ref, part_got, final_ref) = refs[17:24]
    (own_sem, share_send, share_recv, table_send, table_recv, part_send, part_recv, final_send, final_recv) = refs[24:]
    step, steps = pl.program_id(0), pl.num_programs(0)
    hid, inp = lax.axis_index("hid"), lax.axis_index("inp")
    cols = idx_ref.shape[1]
    rows = ENTRIES // n_hid
    peers = [(k, lax.rem(hid + k, n_hid)) for k in range(1, n_hid)]
    mates = [(k, lax.rem(inp + k, n_inp)) for k in range(1, n_inp)]

    def copies():
        out = []
        for k, peer in peers:
            out.append(pltpu.make_async_remote_copy(
                src_ref=shares_ref.at[peer], dst_ref=got_ref.at[k - 1], send_sem=share_send.at[k - 1],
                recv_sem=share_recv.at[k - 1], device_id={"hid": peer}, device_id_type=pl.DeviceIdType.MESH))
        for k, mate in mates:
            for t, (src, dst) in enumerate(((gate_ref, gate_got), (up_ref, up_got))):
                out.append(pltpu.make_async_remote_copy(
                    src_ref=src, dst_ref=dst.at[k - 1], send_sem=table_send.at[2 * (k - 1) + t],
                    recv_sem=table_recv.at[2 * (k - 1) + t], device_id={"inp": mate},
                    device_id_type=pl.DeviceIdType.MESH))
        return out

    def own_copy():
        return pltpu.make_async_copy(shares_ref.at[hid], own_ref, own_sem)

    def lanes_of(tile):
        return pl.ds(pl.multiple_of(tile * cols, LANES), cols)

    late = min(LATE_TILES, tiles)
    groups = [(0, (tiles - late) * cols), ((tiles - late) * cols, late * cols)]

    def part_copy(g, k, peer):
        lanes = pl.ds(*groups[g])
        return pltpu.make_async_remote_copy(
            src_ref=part_ref.at[peer, :, lanes], dst_ref=part_got.at[k - 1, :, lanes],
            send_sem=part_send.at[g, k - 1], recv_sem=part_recv.at[g, k - 1], device_id={"hid": peer},
            device_id_type=pl.DeviceIdType.MESH)

    def final_copy(g, k, peer):
        own = final_ref.at[hid, :, pl.ds(*groups[g])]
        return pltpu.make_async_remote_copy(
            src_ref=own, dst_ref=own, send_sem=final_send.at[g, k - 1], recv_sem=final_recv.at[g, k - 1],
            device_id={"hid": peer}, device_id_type=pl.DeviceIdType.MESH)

    def send(g):
        for k, peer in peers:
            part_copy(g, k, peer).start()

    def settle(g):
        for k, peer in peers:
            part_copy(g, k, peer).wait()
        lanes = pl.ds(*groups[g])
        total = part_ref[hid, :, lanes]
        for k, _ in peers:
            total = total + part_got[k - 1, :, lanes]
        final_ref[hid, :, lanes] = total
        for k, peer in peers:
            final_copy(g, k, peer).start()

    @pl.when(step == 0)
    def _():
        barrier = pltpu.get_barrier_semaphore()
        for _, peer in peers:
            pl.semaphore_signal(barrier, inc=1, device_id={"hid": peer}, device_id_type=pl.DeviceIdType.MESH)
        for _, mate in mates:
            pl.semaphore_signal(barrier, inc=1, device_id={"inp": mate}, device_id_type=pl.DeviceIdType.MESH)
        pl.semaphore_wait(barrier, n_hid + n_inp - 2)
        for copy in copies():
            copy.start()
        own_copy().start()
        take_totals(left_ref, total_ref)

    if tiles > late:

        @pl.when(step == tiles - late)
        def _():
            send(0)

        @pl.when(step == tiles - late // 2)
        def _():
            settle(0)

    part_ref[0, 0:1, lanes_of(step)] = empty_sum(right_ref, total_ref)
    bins_tile(left_ref, right_ref, idx_ref, sign_ref, ones_ref, acc_ref, values, leaf_ref)
    for k in range(1, ENTRIES):
        part_ref[k // rows, k % rows : k % rows + 1, lanes_of(step)] = acc_ref[k : k + 1, :]

    @pl.when(step == steps - 1)
    def _():
        send(1)
        for copy in copies():
            copy.wait()
        own_copy().wait()
        for out, own, got in ((gate_out, gate_ref, gate_got), (up_out, up_ref, up_got)):
            total = own[...]
            for k, _ in mates:
                total = total + got[k - 1]
            out[...] = total
        count, _, block = own_ref.shape
        for i in range(count):
            total = own_ref[i].astype(F32)
            for k, _ in peers:
                total = total + got_ref[k - 1, i].astype(F32)
            grad_out[i] = total
        settle(1)
        for g in range(2):
            if groups[g][1]:
                for k, peer in peers:
                    final_copy(g, k, peer).wait()
        out_ref[...] = final_ref[...]


def finish_kernel(
    scale, down_ref, gate_ref, up_ref, grad_ref, order_ref, signs_ref, down_out, gate_out, up_out, grad_out, down_all
):
    groups, rows, _ = down_ref.shape
    for k in range(groups):
        down_all[k * rows : (k + 1) * rows, :] = down_ref[k]
    for sums, out in ((down_all, down_out), (gate_ref, gate_out), (up_ref, up_out)):
        out[...] = scale * jnp.dot(
            signs_ref[...], sums[...], precision=lax.Precision.HIGHEST, preferred_element_type=F32
        )
    count, _, block = grad_ref.shape
    for i in range(count):
        grad_out[:, i * block : (i + 1) * block] = contract_cols(
            grad_ref[i].astype(BF16), order_ref[...]
        ).astype(BF16)


def finish(down, gate, up, grad, order, scale):
    count, rows, block = grad.shape
    return pl.pallas_call(
        functools.partial(finish_kernel, scale),
        out_shape=[
            jax.ShapeDtypeStruct((ENTRIES, down.shape[2]), F32),
            jax.ShapeDtypeStruct(gate.shape, F32),
            jax.ShapeDtypeStruct(up.shape, F32),
            jax.ShapeDtypeStruct((rows, count * block), BF16),
        ],
        scratch_shapes=[pltpu.VMEM((ENTRIES, down.shape[2]), F32)],
        cost_estimate=cost(rows * count * block * block, 8 * gate.size),
        name="finish",
    )(down, gate, up, grad, order, entry_signs())


def entry_signs():
    both = np.arange(ENTRIES)[:, None] & np.arange(ENTRIES)[None, :]
    odd = sum(both >> bit & 1 for bit in range(4)) & 1
    return jnp.asarray(1 - 2 * odd, F32)


def sign_table():
    entry = np.arange(ENTRIES)[None, :, None]
    sign = 1 - 2 * (entry >> np.arange(4)[:, None, None] & 1)
    return jnp.asarray(np.tile(sign, (1, 1, LANES)).reshape(4 * ENTRIES, LANES), BF16)


def group_ones():
    row = np.arange(ENTRIES)[:, None]
    return jnp.asarray(row == np.arange(ENTRIES * SUB)[None, :] // SUB, BF16)


def grad_bins(left, hidden, gate_index, up_index, gate_table, up_table, shares):
    count, block, tokens = left.shape
    words, width = gate_index.shape
    size, _, rows, _ = hidden.shape
    cols = divisor(width, 256)
    index = pl.BlockSpec((words, cols), lambda j: (0, j))
    table = pl.BlockSpec((ENTRIES, cols), lambda j: (0, j))
    grad = (shares, count, tokens // shares, block)
    return pl.pallas_call(
        grad_kernel,
        grid=(width // cols,),
        in_specs=[
            fixed((count, block, tokens)),
            pl.BlockSpec((size, 1, rows, cols), lambda j: (0, 0, 0, j)),
            pl.BlockSpec((size, 1, rows, cols), lambda j: (0, 1, 0, j)),
            index,
            index,
            fixed((4 * ENTRIES, LANES)),
            fixed((ENTRIES, ENTRIES * SUB)),
            table,
            table,
        ],
        out_specs=[table, table, fixed(grad)],
        out_shape=[
            jax.ShapeDtypeStruct((ENTRIES, width), F32),
            jax.ShapeDtypeStruct((ENTRIES, width), F32),
            jax.ShapeDtypeStruct(grad, BF16),
        ],
        scratch_shapes=[pltpu.VMEM((tokens, cols), BF16)] * 2
        + [pltpu.VMEM((ENTRIES, cols), F32)] * 2
        + [pltpu.VMEM((block, cols), F32)] * 2
        + [pltpu.VMEM((ENTRIES * SUB, cols), BF16)]
        + [pltpu.VMEM((count, tokens, block), F32), pltpu.VMEM((SUB, tokens), BF16)],
        cost_estimate=cost(80 * tokens * words * width, 8 * words * width),
        name="grad_bins",
    )(
        left, hidden, hidden, gate_index, up_index, sign_table(), group_ones(), gate_table, up_table
    )


def down_bins(left, right, index, gate_part, up_part, shares):
    count, block, tokens = left.shape
    words, width = index.shape
    n_hid, n_inp = lax.axis_size("hid"), lax.axis_size("inp")
    cols = divisor(width, 256)
    steps = width // cols
    table = gate_part.shape
    share = shares.shape[1:]
    specs = [
        fixed((count, block, tokens)),
        pl.BlockSpec((tokens, cols), lambda j: (0, j)),
        pl.BlockSpec((words, cols), lambda j: (0, j)),
        fixed((4 * ENTRIES, LANES)),
        fixed((ENTRIES, ENTRIES * SUB)),
        fixed(table),
        fixed(table),
        pl.BlockSpec(memory_space=pl.ANY),
    ]
    args = [left, right, index, sign_table(), group_ones(), gate_part, up_part, shares]
    rows = ENTRIES // n_hid
    groups = (n_hid, rows, width)
    scratch = [
        pltpu.VMEM((SUB, tokens), BF16),
        pltpu.VMEM((ENTRIES, cols), F32),
        pltpu.VMEM((block, cols), F32),
        pltpu.VMEM((block, cols), F32),
        pltpu.VMEM((ENTRIES * SUB, cols), BF16),
        pltpu.VMEM(share, BF16),
        pltpu.VMEM((n_hid - 1,) + share, BF16),
        pltpu.VMEM((n_inp - 1,) + table, F32),
        pltpu.VMEM((n_inp - 1,) + table, F32),
        pltpu.VMEM(groups, F32),
        pltpu.VMEM((n_hid - 1, rows, width), F32),
        pltpu.VMEM(groups, F32),
        pltpu.SemaphoreType.DMA(()),
        pltpu.SemaphoreType.DMA((n_hid - 1,)),
        pltpu.SemaphoreType.DMA((n_hid - 1,)),
        pltpu.SemaphoreType.DMA((2 * (n_inp - 1),)),
        pltpu.SemaphoreType.DMA((2 * (n_inp - 1),)),
        pltpu.SemaphoreType.DMA((2, n_hid - 1)),
        pltpu.SemaphoreType.DMA((2, n_hid - 1)),
        pltpu.SemaphoreType.DMA((2, n_hid - 1)),
        pltpu.SemaphoreType.DMA((2, n_hid - 1)),
    ]
    return pl.pallas_call(
        functools.partial(down_bins_kernel, n_hid, n_inp, steps),
        grid=(steps,),
        in_specs=specs,
        out_specs=[fixed(groups), fixed(table), fixed(table), fixed(share)],
        out_shape=[
            jax.ShapeDtypeStruct(groups, F32),
            jax.ShapeDtypeStruct(table, F32),
            jax.ShapeDtypeStruct(table, F32),
            jax.ShapeDtypeStruct(share, F32),
        ],
        scratch_shapes=scratch,
        compiler_params=pltpu.CompilerParams(collective_id=0, has_side_effects=True),
        cost_estimate=cost(40 * tokens * words * width, 4 * words * width),
        name="down_bins",
    )(*args)


def pairing(block, dtype):
    row = np.arange(block)[:, None]
    col = np.arange(block)[None, :]
    half = block // 2
    return jnp.asarray(row == 2 * (col % half) + col // half, dtype)


def to_blocks(array):
    rows, cols = array.shape
    block = math.gcd(cols, 256)
    out = lax.dot_general(
        array.reshape(rows, cols // block, block), pairing(block, array.dtype), (((2,), (0,)), ((), ())),
        preferred_element_type=F32,
    )
    return jnp.swapaxes(out.astype(array.dtype), 0, 1)


def shards(inputs, out_grad, gate_index, up_index, down_index, gate_table, up_table, down_table):
    tokens = inputs.shape[0]
    width = gate_index.shape[1]
    x_blocks = to_blocks(inputs)
    order = pairing(x_blocks.shape[2], BF16)
    hidden = hidden_grads(
        x_blocks, out_grad, gate_index, up_index, down_index, gate_table, up_table, down_table,
        pairing(math.gcd(width, 256), BF16),
    )
    x_turned = jnp.swapaxes(x_blocks, 1, 2)
    block = math.gcd(width, 256)
    acts = hidden[:, 2].reshape(tokens, width // block, block)
    gate_part, up_part, shares = grad_bins(
        x_turned, hidden, gate_index, up_index, gate_table, up_table, lax.axis_size("hid")
    )
    sums = down_bins(jnp.transpose(acts, (1, 2, 0)), out_grad, down_index, gate_part, up_part, shares)
    down_sum, gate_sum, up_sum, input_grad = finish(*sums, order, 1.0 / (tokens * ENTRIES))
    return input_grad, gate_sum, up_sum, down_sum


def solution(mesh):
    in_specs = (
        P(None, "inp"),
        P(None, "inp"),
        P("inp", "hid"),
        P("inp", "hid"),
        P("hid", "inp"),
        P(None, "hid"),
        P(None, "hid"),
        P(None, "inp"),
    )
    out_specs = (P("hid", "inp"), P(None, "hid"), P(None, "hid"), P(None, "inp"))
    return jax.shard_map(shards, mesh=mesh, in_specs=in_specs, out_specs=out_specs, check_vma=False)
```

```python
import functools
import math

import jax
import jax.numpy as jnp
import numpy as np
from jax import lax
from jax.experimental import pallas as pl
from jax.experimental.pallas import tpu as pltpu
from jax.sharding import PartitionSpec as P

LANES = 128
SUB = 16
ENTRIES = 16
F32 = jnp.float32
BF16 = jnp.bfloat16
LOOKUP = lax.GatherDimensionNumbers(
    offset_dims=(), collapsed_slice_dims=(0,), start_index_map=(0,),
    operand_batching_dims=(1,), start_indices_batching_dims=(1,),
)


def divisor(size, most, unit=LANES):
    best = unit
    for cand in range(unit, most + 1, unit):
        if size % cand == 0:
            best = cand
    return best


def cost(flops, nbytes):
    return pl.CostEstimate(flops=int(flops), bytes_accessed=int(nbytes), transcendentals=0)


def look_up(table, index):
    return lax.gather(
        table, index[..., None], LOOKUP, (1, 1), mode=lax.GatherScatterMode.PROMISE_IN_BOUNDS
    )


def nibbles(words):
    words = words.astype(jnp.int16)
    return jnp.bitwise_and(words, jnp.int16(15)), lax.shift_right_logical(words, jnp.int16(4))


def fixed(shape):
    return pl.BlockSpec(shape, lambda j: (0,) * len(shape))


def lane_chunks(cols):
    return [slice(c * LANES, (c + 1) * LANES) for c in range(cols // LANES)]


def tables_of(table_ref):
    return [table_ref[:, lanes].astype(BF16) for lanes in lane_chunks(table_ref.shape[1])]


def decode_block(idx_ref, tables, i, half):
    columns = []
    for lanes, table in zip(lane_chunks(idx_ref.shape[1]), tables):
        pieces = [[], []]
        for step in range(half // SUB):
            row = pl.multiple_of(i * half + step * SUB, SUB)
            for piece, index in zip(pieces, nibbles(idx_ref[pl.ds(row, SUB), lanes])):
                piece.append(look_up(table, index))
        columns.append(jnp.concatenate(pieces[0] + pieces[1], axis=0))
    return jnp.concatenate(columns, axis=1)


def contract_cols(left, right):
    return lax.dot_general(left, right, (((1,), (1,)), ((), ())), preferred_element_type=F32)


def grouped(count, most, body):
    size = min(count, most)

    def step(j, carry):
        body(j * size, size)
        return carry

    lax.fori_loop(0, count // size, step, 0)
    if count % size:
        body(count - count % size, count % size)


LATE_TILES = 4
LAG_CHIP = 1
LAG_HIDDEN = 3
LAG_RELAY = 5
HIDDEN_FROM = 5
RELAY_FROM = 7


def mesh_copy(src, dst, send, recv, **device):
    return pltpu.make_async_remote_copy(
        src_ref=src, dst_ref=dst, send_sem=send, recv_sem=recv, device_id=device,
        device_id_type=pl.DeviceIdType.MESH,
    )


def repeat(first, last, body):
    def step(i, carry):
        body(i)
        return carry

    lax.fori_loop(first, last, step, 0)


def hidden_kernel(size, down_steps, *refs):
    (og_ref, x_ref, down_ref, down_table, gate_ref, gate_table, up_ref, up_table, order_ref) = refs[:9]
    (out_ref, hid_acc, hid_part, hid_sib, hid_chip, hid_got, part, sib, chip, chip_got, all_ref) = refs[9:20]
    (hid_send, hid_recv, hid_chip_send, hid_chip_recv, sib_send, sib_recv) = refs[20:26]
    (chip_send, chip_recv, pair_send, pair_recv, far_send, far_recv, relay_send, relay_recv) = refs[26:]
    step, steps = pl.program_id(0), pl.num_programs(0)
    count, _, block = x_ref.shape
    hid_count, tokens, cols = hid_acc.shape
    tiles = hid_count
    chips = size // 2
    rows = tokens // size
    me = lax.axis_index("inp")
    my_chip, side = me // 2, lax.rem(me, 2)
    other = 1 - side
    sibling = 2 * my_chip + other
    far = [(k, lax.rem(my_chip + k, chips)) for k in range(1, chips)]

    def lanes_of(tile):
        return pl.ds(pl.multiple_of(tile * cols, LANES), cols)

    def hid_copy():
        return mesh_copy(hid_part.at[other], hid_sib, hid_send, hid_recv, inp=sibling)

    def hid_far(k, there):
        return mesh_copy(
            hid_chip.at[there], hid_got.at[k - 1], hid_chip_send.at[k - 1], hid_chip_recv.at[k - 1],
            inp=2 * there + side,
        )

    def sib_copy(a, tile):
        lanes = lanes_of(tile)
        return mesh_copy(
            part.at[a, other, :, :, lanes], sib.at[a, :, :, lanes], sib_send.at[a, tile], sib_recv.at[a, tile],
            inp=sibling,
        )

    def chip_copy(a, tile, k, there):
        lanes = lanes_of(tile)
        return mesh_copy(
            chip.at[a, there, :, lanes], chip_got.at[a, k - 1, :, lanes], chip_send.at[a, tile, k - 1],
            chip_recv.at[a, tile, k - 1], inp=2 * there + side,
        )

    def pair_copy(tile):
        own = all_ref.at[me, :, :, lanes_of(tile)]
        return mesh_copy(own, own, pair_send.at[tile], pair_recv.at[tile], inp=sibling)

    def far_copy(tile, k, there):
        own = all_ref.at[me, :, :, lanes_of(tile)]
        return mesh_copy(
            own, own, far_send.at[tile, k - 1], far_recv.at[tile, k - 1], inp=2 * there + side
        )

    def relay_copy(tile, k):
        source = 2 * lax.rem(my_chip + chips - k, chips) + side
        theirs = all_ref.at[source, :, :, lanes_of(tile)]
        return mesh_copy(theirs, theirs, relay_send.at[tile, k - 1], relay_recv.at[tile, k - 1], inp=sibling)

    def hid_sum():
        hid_copy().wait_recv()
        for c in range(chips):
            for i in range(hid_count):
                hid_chip[c, i] = (hid_part[side, c, i].astype(F32) + hid_sib[c, i].astype(F32)).astype(BF16)
        for k, there in far:
            hid_far(k, there).start()

    def chip_sum(tile):
        for a in range(2):
            chip_part(a, tile)

    def chip_part(a, tile):
        lanes = lanes_of(tile)
        sib_copy(a, tile).wait_recv()
        for c in range(chips):
            total = part[a, side, c, :, lanes].astype(F32) + sib[a, c, :, lanes].astype(F32)
            chip[a, c, :, lanes] = total.astype(BF16)
        for k, there in far:
            chip_copy(a, tile, k, there).start()

    def hidden(tile):
        lanes = lanes_of(tile)
        shares = []
        for a in range(2):
            total = chip[a, my_chip, :, lanes].astype(F32)
            for k, there in far:
                chip_copy(a, tile, k, there).wait_recv()
                total = total + chip_got[a, k - 1, :, lanes].astype(F32)
            shares.append(total)
        total = hid_chip[my_chip, tile].astype(F32)
        for k, _ in far:
            total = total + hid_got[k - 1, tile].astype(F32)
        high = total.astype(BF16)
        low = (total - high.astype(F32)).astype(BF16)
        grad = contract_cols(high, order_ref[...]) + contract_cols(low, order_ref[...])
        gate_grad, up_grad, activ = local_hidden(shares[0], shares[1], grad)
        all_ref[me, 0, :, lanes] = gate_grad
        all_ref[me, 1, :, lanes] = up_grad
        all_ref[me, 2, :, lanes] = jnp.dot(activ, order_ref[...], preferred_element_type=F32).astype(BF16)
        pair_copy(tile).start()
        for k, there in far:
            far_copy(tile, k, there).start()

    def relay(tile):
        for k, there in far:
            far_copy(tile, k, there).wait_recv()
            relay_copy(tile, k).start()

    @pl.when(step == 0)
    def _():
        barrier = pltpu.get_barrier_semaphore()
        pl.semaphore_signal(barrier, inc=1, device_id={"inp": sibling}, device_id_type=pl.DeviceIdType.MESH)
        for _, there in far:
            pl.semaphore_signal(
                barrier, inc=1, device_id={"inp": 2 * there + side}, device_id_type=pl.DeviceIdType.MESH
            )
        pl.semaphore_wait(barrier, chips)
        hid_acc[...] = jnp.zeros_like(hid_acc)

    unit = step - down_steps - LAG_CHIP

    @pl.when(unit >= 0)
    def _():
        chip_sum(unit)

    turn = step - down_steps

    @pl.when(turn == HIDDEN_FROM)
    def _():
        for k, there in far:
            hid_far(k, there).wait_recv()

    @pl.when(turn >= HIDDEN_FROM)
    def _():
        now = turn - LAG_HIDDEN
        repeat(jnp.where(turn == HIDDEN_FROM, 0, now), now + 1, hidden)

    @pl.when(turn >= RELAY_FROM)
    def _():
        now = turn - LAG_RELAY
        repeat(jnp.where(turn == RELAY_FROM, 0, now), now + 1, relay)

    @pl.when(step < down_steps)
    def _():
        tables = tables_of(down_table)

        def body(first, n):
            for k in range(n):
                hid_acc[first + k] += contract_cols(
                    og_ref[...], decode_block(down_ref, tables, first + k, cols // 2)
                )

        grouped(hid_count, 13, body)

    @pl.when(step == down_steps - 1)
    def _():
        for c in range(chips):
            for s in range(2):
                first = (2 * c + s) * rows
                for i in range(hid_count):
                    hid_part[s, c, i] = hid_acc[i, first : first + rows, :].astype(BF16)
        hid_copy().start()

    def product(tile):
        tables = tables_of(gate_table), tables_of(up_table)
        pre = hid_acc.at[0], hid_acc.at[1]
        for pre_ref in pre:
            pre_ref[...] = jnp.zeros_like(pre_ref)

        def body(first, n):
            for a, idx_ref in enumerate((gate_ref, up_ref)):
                pre[a][...] += sum(
                    jnp.dot(
                        x_ref[first + k], decode_block(idx_ref, tables[a], first + k, block // 2),
                        preferred_element_type=F32,
                    )
                    for k in range(n)
                )

        grouped(count, 16, body)
        for a in range(2):
            for c in range(chips):
                for s in range(2):
                    first = (2 * c + s) * rows
                    part[a, s, c, :, lanes_of(tile)] = pre[a][first : first + rows, :].astype(BF16)
            sib_copy(a, tile).start()

    @pl.when(step >= down_steps)
    def _():
        product(step - down_steps)

    @pl.when(turn == 0)
    def _():
        hid_sum()

    @pl.when(step == steps - 1)
    def _():
        repeat(tiles - LAG_CHIP, tiles, chip_sum)
        repeat(tiles - LAG_HIDDEN, tiles, hidden)
        repeat(tiles - LAG_RELAY, tiles, relay)
        hid_copy().wait_send()
        for k, there in far:
            hid_far(k, there).wait_send()

        def finish_tile(tile):
            for a in range(2):
                sib_copy(a, tile).wait_send()
                for k, there in far:
                    chip_copy(a, tile, k, there).wait_send()
            pair_copy(tile).wait()
            for k, there in far:
                far_copy(tile, k, there).wait_send()
                relay_copy(tile, k).wait()

        repeat(0, tiles, finish_tile)
        out_ref[...] = all_ref[...]


def hidden_grads(x_blocks, out_grad, gate_index, up_index, down_index, gate_table, up_table, down_table, order):
    count, tokens, block = x_blocks.shape
    words, width = gate_index.shape
    down_words, model = down_index.shape
    size = lax.axis_size("inp")
    chips, rows = size // 2, tokens // size
    cols = math.gcd(width, 256)
    tiles = width // cols
    wide = divisor(model, 512)
    down_steps = model // wide
    gathered = (size, 3, rows, width)

    def at(first, last):
        return lambda j: (0, jnp.clip(j - first, 0, last - 1))

    blocks = (tiles, rows, cols)
    dma = pltpu.SemaphoreType.DMA
    return pl.pallas_call(
        functools.partial(hidden_kernel, size, down_steps),
        grid=(down_steps + tiles,),
        in_specs=[
            pl.BlockSpec((tokens, wide), at(0, down_steps)),
            fixed((count, tokens, block)),
            pl.BlockSpec((down_words, wide), at(0, down_steps)),
            pl.BlockSpec((ENTRIES, wide), at(0, down_steps)),
            pl.BlockSpec((words, cols), at(down_steps, tiles)),
            pl.BlockSpec((ENTRIES, cols), at(down_steps, tiles)),
            pl.BlockSpec((words, cols), at(down_steps, tiles)),
            pl.BlockSpec((ENTRIES, cols), at(down_steps, tiles)),
            fixed(order.shape),
        ],
        out_specs=fixed(gathered),
        out_shape=jax.ShapeDtypeStruct(gathered, BF16),
        scratch_shapes=[
            pltpu.VMEM((tiles, tokens, cols), F32),
            pltpu.VMEM((2, chips) + blocks, BF16),
            pltpu.VMEM((chips,) + blocks, BF16),
            pltpu.VMEM((chips,) + blocks, BF16),
            pltpu.VMEM((chips - 1,) + blocks, BF16),
            pltpu.VMEM((2, 2, chips, rows, width), BF16),
            pltpu.VMEM((2, chips, rows, width), BF16),
            pltpu.VMEM((2, chips, rows, width), BF16),
            pltpu.VMEM((2, chips - 1, rows, width), BF16),
            pltpu.VMEM(gathered, BF16),
            dma(()), dma(()), dma((chips - 1,)), dma((chips - 1,)),
            dma((2, tiles)), dma((2, tiles)), dma((2, tiles, chips - 1)), dma((2, tiles, chips - 1)),
            dma((tiles,)), dma((tiles,)), dma((tiles, chips - 1)), dma((tiles, chips - 1)),
            dma((tiles, chips - 1)), dma((tiles, chips - 1)),
        ],
        compiler_params=pltpu.CompilerParams(collective_id=1, has_side_effects=True),
        cost_estimate=cost(12 * tokens * words * width, 12 * words * width),
        name="hidden_grads",
    )(
        out_grad, x_blocks, down_index, down_table, gate_index, gate_table, up_index, up_table, order
    )


def local_hidden(pre_gate, pre_up, hidden_grad):
    sig_gate = jax.nn.sigmoid(pre_gate)
    silu_gate = pre_gate * sig_gate
    activ = (silu_gate * pre_up).astype(BF16)
    gate_grad = (hidden_grad * pre_up * sig_gate * (1.0 + pre_gate * (1.0 - sig_gate))).astype(BF16)
    up_grad = (hidden_grad * silu_gate).astype(BF16)
    return gate_grad, up_grad, activ


def signed_sums(sums, value, signs):
    out = [None] * ENTRIES

    def walk(part, bits, chosen):
        if chosen:
            out[chosen] = part if sums is None else sums[chosen - 1] + part
        for bit in range(bits):
            walk(signs[bit] * part, bit, chosen | 1 << bit)

    walk(value, len(signs), 0)
    return out[1:]


def start_bins(accs, leaf_ref):
    for acc_ref in accs:
        acc_ref[...] = jnp.zeros_like(acc_ref)
    leaf_ref[...] = jnp.zeros_like(leaf_ref)


def make_values(left_ref, right_ref, i, value_ref):
    value_ref[...] = jnp.dot(left_ref[i], right_ref[...], preferred_element_type=F32)


def add_signed(idx_ref, signs, i, value_ref, tables=None):
    half = value_ref.shape[0] // 2
    leaves, weights = [], []
    for c, lanes in enumerate(lane_chunks(idx_ref.shape[1])):
        runs, sums, pieces = [], None, ([], [])
        for step in range(half // SUB):
            row = pl.multiple_of(i * half + step * SUB, SUB)
            for parity, index in enumerate(nibbles(idx_ref[pl.ds(row, SUB), lanes])):
                first = parity * half + step * SUB
                if tables is not None:
                    pieces[parity].append(look_up(tables[c], index))
                value = value_ref[first : first + SUB, lanes].astype(BF16)
                sums = signed_sums(sums, value, [look_up(sign, index) for sign in signs])
            if step % 4 == 3 or step == half // SUB - 1:
                runs.append(sums)
                sums = None
        while len(runs) > 1:
            runs = [[a + b for a, b in zip(*runs[:2])]] + runs[2:]
        leaves.append(runs[0])
        if tables is not None:
            weights.append(jnp.concatenate(pieces[0] + pieces[1], axis=0))
    return leaves, jnp.concatenate(weights, axis=1) if weights else None


def keep_leaves(leaves, leaf_ref):
    for c, sums in enumerate(leaves):
        for a, total in enumerate(sums):
            leaf_ref[SUB * (a + 1) : SUB * (a + 2), c * LANES : (c + 1) * LANES] = total


def close_now(ones_ref, leaves, acc_ref):
    blank = jnp.zeros((SUB, LANES), BF16)
    whole = jnp.concatenate([jnp.concatenate([blank] + sums, axis=0) for sums in leaves], axis=1)
    acc_ref[...] += jnp.dot(ones_ref[...], whole, preferred_element_type=F32)


def close_block(ones_ref, leaf_ref, acc_ref):
    acc_ref[...] += jnp.dot(ones_ref[...], leaf_ref[...], preferred_element_type=F32)


def take_totals(left_ref, total_ref):
    count, block, tokens = left_ref.shape
    totals = [jnp.zeros((8, tokens), F32)] * 8
    for i in range(count):
        for first in range(0, block, SUB):
            rows = left_ref[i, first : first + SUB, :].astype(F32)
            k = first // SUB % 4 * 2
            totals[k : k + 2] = totals[k] + rows[:8], totals[k + 1] + rows[8:]
    total = sum(totals)
    rest = jnp.broadcast_to(jnp.sum(total, axis=0, keepdims=True), total_ref.shape)
    row = lax.broadcasted_iota(jnp.int32, total_ref.shape, 0)
    parts = jnp.zeros(total_ref.shape, F32)
    for k in range(3):
        part = rest.astype(BF16).astype(F32)
        parts = jnp.where(row == k, part, parts)
        rest = rest - part
    total_ref[...] = parts.astype(BF16)


def empty_sum(right_ref, total_ref):
    whole = jnp.dot(total_ref[...], right_ref[...], preferred_element_type=F32)
    return whole[:1] + whole[1:2] + whole[2:3]


def signs_of(sign_ref):
    return [sign_ref[SUB * b : SUB * b + SUB, :] for b in range(4)]


def bins_tile(left_ref, right_ref, idx_ref, sign_ref, ones_ref, acc_ref, values, leaf_ref):
    count = left_ref.shape[0]
    signs = signs_of(sign_ref)
    start_bins([acc_ref], leaf_ref)
    make_values(left_ref, right_ref, 0, values[0])

    def body(j, carry):
        close_block(ones_ref, leaf_ref, acc_ref)
        make_values(left_ref, right_ref, 2 * j + 1, values[1])
        leaves, _ = add_signed(idx_ref, signs, 2 * j, values[0])
        close_now(ones_ref, leaves, acc_ref)
        make_values(left_ref, right_ref, jnp.minimum(2 * j + 2, count - 1), values[0])
        leaves, _ = add_signed(idx_ref, signs, 2 * j + 1, values[1])
        keep_leaves(leaves, leaf_ref)
        return carry

    lax.fori_loop(0, count // 2, body, 0)
    close_block(ones_ref, leaf_ref, acc_ref)
    if count % 2:
        leaves, _ = add_signed(idx_ref, signs, count - 1, values[0])
        close_now(ones_ref, leaves, acc_ref)


def grad_kernel(
    left_ref, gate_hidden, up_hidden, gate_idx, up_idx, sign_ref, ones_ref, gate_table, up_table,
    gate_out, up_out, share_ref, gate_ref, up_ref, gate_acc, up_acc, gate_value, up_value, grad_ref,
    total_ref,
):
    count, block, _ = left_ref.shape
    half = block // 2
    size, _, per, _ = gate_hidden.shape
    signs = signs_of(sign_ref)
    tables = tables_of(gate_table), tables_of(up_table)

    @pl.when(pl.program_id(0) == 0)
    def _():
        grad_ref[...] = jnp.zeros_like(grad_ref)
        take_totals(left_ref, total_ref)

    for p in range(size):
        gate_ref[p * per : (p + 1) * per, :] = gate_hidden[p, 0]
        up_ref[p * per : (p + 1) * per, :] = up_hidden[p, 0]
    gate_out[0:1, :] = empty_sum(gate_ref, total_ref)
    up_out[0:1, :] = empty_sum(up_ref, total_ref)
    gate_acc[...] = jnp.zeros_like(gate_acc)
    up_acc[...] = jnp.zeros_like(up_acc)
    make_values(left_ref, gate_ref, 0, gate_value)

    def close_up(i, leaves, weights):
        close_now(ones_ref, leaves, up_acc)
        grad_ref[i] += contract_cols(up_ref[...], weights)

    def body(i, carry):
        close_up(jnp.maximum(i - 1, 0), *carry)
        make_values(left_ref, up_ref, i, up_value)
        leaves, weights = add_signed(gate_idx, signs, i, gate_value, tables[0])
        close_now(ones_ref, leaves, gate_acc)
        grad_ref[i] += contract_cols(gate_ref[...], weights)
        make_values(left_ref, gate_ref, jnp.minimum(i + 1, count - 1), gate_value)
        return add_signed(up_idx, signs, i, up_value, tables[1])

    cols = up_ref.shape[1]
    blank = [[jnp.zeros((SUB, LANES), BF16)] * (ENTRIES - 1)] * (cols // LANES)
    last = lax.fori_loop(0, count, body, (blank, jnp.zeros((block, cols), BF16)))
    close_up(count - 1, *last)
    for out, acc_ref in ((gate_out, gate_acc), (up_out, up_acc)):
        out[1:, :] = acc_ref[1:, :]

    @pl.when(pl.program_id(0) == pl.num_programs(0) - 1)
    def _():
        shares, _, rows, _ = share_ref.shape
        for p in range(shares):
            share_ref[p] = grad_ref[:, p * rows : (p + 1) * rows, :].astype(BF16)


def down_bins_kernel(n_hid, n_inp, tiles, *refs):
    (left_ref, right_ref, idx_ref, sign_ref, ones_ref, gate_ref, up_ref, shares_ref) = refs[:8]
    out_ref, gate_out, up_out, grad_out = refs[8:12]
    total_ref, acc_ref, values, leaf_ref = refs[12], refs[13], refs[14:16], refs[16]
    (own_ref, got_ref, gate_got, up_got, part_ref, part_got, final_ref) = refs[17:24]
    (own_sem, share_send, share_recv, table_send, table_recv, part_send, part_recv, final_send, final_recv) = refs[24:]
    step, steps = pl.program_id(0), pl.num_programs(0)
    hid, inp = lax.axis_index("hid"), lax.axis_index("inp")
    cols = idx_ref.shape[1]
    rows = ENTRIES // n_hid
    peers = [(k, lax.rem(hid + k, n_hid)) for k in range(1, n_hid)]
    mates = [(k, lax.rem(inp + k, n_inp)) for k in range(1, n_inp)]

    def copies():
        out = []
        for k, peer in peers:
            out.append(pltpu.make_async_remote_copy(
                src_ref=shares_ref.at[peer], dst_ref=got_ref.at[k - 1], send_sem=share_send.at[k - 1],
                recv_sem=share_recv.at[k - 1], device_id={"hid": peer}, device_id_type=pl.DeviceIdType.MESH))
        for k, mate in mates:
            for t, (src, dst) in enumerate(((gate_ref, gate_got), (up_ref, up_got))):
                out.append(pltpu.make_async_remote_copy(
                    src_ref=src, dst_ref=dst.at[k - 1], send_sem=table_send.at[2 * (k - 1) + t],
                    recv_sem=table_recv.at[2 * (k - 1) + t], device_id={"inp": mate},
                    device_id_type=pl.DeviceIdType.MESH))
        return out

    def own_copy():
        return pltpu.make_async_copy(shares_ref.at[hid], own_ref, own_sem)

    def lanes_of(tile):
        return pl.ds(pl.multiple_of(tile * cols, LANES), cols)

    late = min(LATE_TILES, tiles)
    groups = [(0, (tiles - late) * cols), ((tiles - late) * cols, late * cols)]

    def part_copy(g, k, peer):
        lanes = pl.ds(*groups[g])
        return pltpu.make_async_remote_copy(
            src_ref=part_ref.at[peer, :, lanes], dst_ref=part_got.at[k - 1, :, lanes],
            send_sem=part_send.at[g, k - 1], recv_sem=part_recv.at[g, k - 1], device_id={"hid": peer},
            device_id_type=pl.DeviceIdType.MESH)

    def final_copy(g, k, peer):
        own = final_ref.at[hid, :, pl.ds(*groups[g])]
        return pltpu.make_async_remote_copy(
            src_ref=own, dst_ref=own, send_sem=final_send.at[g, k - 1], recv_sem=final_recv.at[g, k - 1],
            device_id={"hid": peer}, device_id_type=pl.DeviceIdType.MESH)

    def send(g):
        for k, peer in peers:
            part_copy(g, k, peer).start()

    def settle(g):
        for k, peer in peers:
            part_copy(g, k, peer).wait()
        lanes = pl.ds(*groups[g])
        total = part_ref[hid, :, lanes]
        for k, _ in peers:
            total = total + part_got[k - 1, :, lanes]
        final_ref[hid, :, lanes] = total
        for k, peer in peers:
            final_copy(g, k, peer).start()

    @pl.when(step == 0)
    def _():
        barrier = pltpu.get_barrier_semaphore()
        for _, peer in peers:
            pl.semaphore_signal(barrier, inc=1, device_id={"hid": peer}, device_id_type=pl.DeviceIdType.MESH)
        for _, mate in mates:
            pl.semaphore_signal(barrier, inc=1, device_id={"inp": mate}, device_id_type=pl.DeviceIdType.MESH)
        pl.semaphore_wait(barrier, n_hid + n_inp - 2)
        for copy in copies():
            copy.start()
        own_copy().start()
        take_totals(left_ref, total_ref)

    if tiles > late:

        @pl.when(step == tiles - late)
        def _():
            send(0)

        @pl.when(step == tiles - late // 2)
        def _():
            settle(0)

    part_ref[0, 0:1, lanes_of(step)] = empty_sum(right_ref, total_ref)
    bins_tile(left_ref, right_ref, idx_ref, sign_ref, ones_ref, acc_ref, values, leaf_ref)
    for k in range(1, ENTRIES):
        part_ref[k // rows, k % rows : k % rows + 1, lanes_of(step)] = acc_ref[k : k + 1, :]

    @pl.when(step == steps - 1)
    def _():
        send(1)
        for copy in copies():
            copy.wait()
        own_copy().wait()
        for out, own, got in ((gate_out, gate_ref, gate_got), (up_out, up_ref, up_got)):
            total = own[...]
            for k, _ in mates:
                total = total + got[k - 1]
            out[...] = total
        count, _, block = own_ref.shape
        for i in range(count):
            total = own_ref[i].astype(F32)
            for k, _ in peers:
                total = total + got_ref[k - 1, i].astype(F32)
            grad_out[i] = total
        settle(1)
        for g in range(2):
            if groups[g][1]:
                for k, peer in peers:
                    final_copy(g, k, peer).wait()
        out_ref[...] = final_ref[...]


def finish_kernel(
    scale, down_ref, gate_ref, up_ref, grad_ref, order_ref, signs_ref, down_out, gate_out, up_out, grad_out, down_all
):
    groups, rows, _ = down_ref.shape
    for k in range(groups):
        down_all[k * rows : (k + 1) * rows, :] = down_ref[k]
    for sums, out in ((down_all, down_out), (gate_ref, gate_out), (up_ref, up_out)):
        out[...] = scale * jnp.dot(
            signs_ref[...], sums[...], precision=lax.Precision.HIGHEST, preferred_element_type=F32
        )
    count, _, block = grad_ref.shape
    for i in range(count):
        grad_out[:, i * block : (i + 1) * block] = contract_cols(
            grad_ref[i].astype(BF16), order_ref[...]
        ).astype(BF16)


def finish(down, gate, up, grad, order, scale):
    count, rows, block = grad.shape
    return pl.pallas_call(
        functools.partial(finish_kernel, scale),
        out_shape=[
            jax.ShapeDtypeStruct((ENTRIES, down.shape[2]), F32),
            jax.ShapeDtypeStruct(gate.shape, F32),
            jax.ShapeDtypeStruct(up.shape, F32),
            jax.ShapeDtypeStruct((rows, count * block), BF16),
        ],
        scratch_shapes=[pltpu.VMEM((ENTRIES, down.shape[2]), F32)],
        cost_estimate=cost(rows * count * block * block, 8 * gate.size),
        name="finish",
    )(down, gate, up, grad, order, entry_signs())


def entry_signs():
    both = np.arange(ENTRIES)[:, None] & np.arange(ENTRIES)[None, :]
    odd = sum(both >> bit & 1 for bit in range(4)) & 1
    return jnp.asarray(1 - 2 * odd, F32)


def sign_table():
    entry = np.arange(ENTRIES)[None, :, None]
    sign = 1 - 2 * (entry >> np.arange(4)[:, None, None] & 1)
    return jnp.asarray(np.tile(sign, (1, 1, LANES)).reshape(4 * ENTRIES, LANES), BF16)


def group_ones():
    row = np.arange(ENTRIES)[:, None]
    return jnp.asarray(row == np.arange(ENTRIES * SUB)[None, :] // SUB, BF16)


def grad_bins(left, hidden, gate_index, up_index, gate_table, up_table, shares):
    count, block, tokens = left.shape
    words, width = gate_index.shape
    size, _, rows, _ = hidden.shape
    cols = divisor(width, 256)
    index = pl.BlockSpec((words, cols), lambda j: (0, j))
    table = pl.BlockSpec((ENTRIES, cols), lambda j: (0, j))
    grad = (shares, count, tokens // shares, block)
    return pl.pallas_call(
        grad_kernel,
        grid=(width // cols,),
        in_specs=[
            fixed((count, block, tokens)),
            pl.BlockSpec((size, 1, rows, cols), lambda j: (0, 0, 0, j)),
            pl.BlockSpec((size, 1, rows, cols), lambda j: (0, 1, 0, j)),
            index,
            index,
            fixed((4 * ENTRIES, LANES)),
            fixed((ENTRIES, ENTRIES * SUB)),
            table,
            table,
        ],
        out_specs=[table, table, fixed(grad)],
        out_shape=[
            jax.ShapeDtypeStruct((ENTRIES, width), F32),
            jax.ShapeDtypeStruct((ENTRIES, width), F32),
            jax.ShapeDtypeStruct(grad, BF16),
        ],
        scratch_shapes=[pltpu.VMEM((tokens, cols), BF16)] * 2
        + [pltpu.VMEM((ENTRIES, cols), F32)] * 2
        + [pltpu.VMEM((block, cols), F32)] * 2
        + [pltpu.VMEM((count, tokens, block), F32), pltpu.VMEM((SUB, tokens), BF16)],
        cost_estimate=cost(80 * tokens * words * width, 8 * words * width),
        name="grad_bins",
    )(
        left, hidden, hidden, gate_index, up_index, sign_table(), group_ones(), gate_table, up_table
    )


def down_bins(left, right, index, gate_part, up_part, shares):
    count, block, tokens = left.shape
    words, width = index.shape
    n_hid, n_inp = lax.axis_size("hid"), lax.axis_size("inp")
    cols = divisor(width, 256)
    steps = width // cols
    table = gate_part.shape
    share = shares.shape[1:]
    specs = [
        fixed((count, block, tokens)),
        pl.BlockSpec((tokens, cols), lambda j: (0, j)),
        pl.BlockSpec((words, cols), lambda j: (0, j)),
        fixed((4 * ENTRIES, LANES)),
        fixed((ENTRIES, ENTRIES * SUB)),
        fixed(table),
        fixed(table),
        pl.BlockSpec(memory_space=pl.ANY),
    ]
    args = [left, right, index, sign_table(), group_ones(), gate_part, up_part, shares]
    rows = ENTRIES // n_hid
    groups = (n_hid, rows, width)
    scratch = [
        pltpu.VMEM((SUB, tokens), BF16),
        pltpu.VMEM((ENTRIES, cols), F32),
        pltpu.VMEM((block, cols), F32),
        pltpu.VMEM((block, cols), F32),
        pltpu.VMEM((ENTRIES * SUB, cols), BF16),
        pltpu.VMEM(share, BF16),
        pltpu.VMEM((n_hid - 1,) + share, BF16),
        pltpu.VMEM((n_inp - 1,) + table, F32),
        pltpu.VMEM((n_inp - 1,) + table, F32),
        pltpu.VMEM(groups, F32),
        pltpu.VMEM((n_hid - 1, rows, width), F32),
        pltpu.VMEM(groups, F32),
        pltpu.SemaphoreType.DMA(()),
        pltpu.SemaphoreType.DMA((n_hid - 1,)),
        pltpu.SemaphoreType.DMA((n_hid - 1,)),
        pltpu.SemaphoreType.DMA((2 * (n_inp - 1),)),
        pltpu.SemaphoreType.DMA((2 * (n_inp - 1),)),
        pltpu.SemaphoreType.DMA((2, n_hid - 1)),
        pltpu.SemaphoreType.DMA((2, n_hid - 1)),
        pltpu.SemaphoreType.DMA((2, n_hid - 1)),
        pltpu.SemaphoreType.DMA((2, n_hid - 1)),
    ]
    return pl.pallas_call(
        functools.partial(down_bins_kernel, n_hid, n_inp, steps),
        grid=(steps,),
        in_specs=specs,
        out_specs=[fixed(groups), fixed(table), fixed(table), fixed(share)],
        out_shape=[
            jax.ShapeDtypeStruct(groups, F32),
            jax.ShapeDtypeStruct(table, F32),
            jax.ShapeDtypeStruct(table, F32),
            jax.ShapeDtypeStruct(share, F32),
        ],
        scratch_shapes=scratch,
        compiler_params=pltpu.CompilerParams(collective_id=0, has_side_effects=True),
        cost_estimate=cost(40 * tokens * words * width, 4 * words * width),
        name="down_bins",
    )(*args)


def pairing(block, dtype):
    row = np.arange(block)[:, None]
    col = np.arange(block)[None, :]
    half = block // 2
    return jnp.asarray(row == 2 * (col % half) + col // half, dtype)


def to_blocks(array):
    rows, cols = array.shape
    block = math.gcd(cols, 256)
    out = lax.dot_general(
        array.reshape(rows, cols // block, block), pairing(block, array.dtype), (((2,), (0,)), ((), ())),
        preferred_element_type=F32,
    )
    return jnp.swapaxes(out.astype(array.dtype), 0, 1)


def shards(inputs, out_grad, gate_index, up_index, down_index, gate_table, up_table, down_table):
    tokens = inputs.shape[0]
    width = gate_index.shape[1]
    x_blocks = to_blocks(inputs)
    order = pairing(x_blocks.shape[2], BF16)
    hidden = hidden_grads(
        x_blocks, out_grad, gate_index, up_index, down_index, gate_table, up_table, down_table,
        pairing(math.gcd(width, 256), BF16),
    )
    x_turned = jnp.swapaxes(x_blocks, 1, 2)
    block = math.gcd(width, 256)
    acts = hidden[:, 2].reshape(tokens, width // block, block)
    gate_part, up_part, shares = grad_bins(
        x_turned, hidden, gate_index, up_index, gate_table, up_table, lax.axis_size("hid")
    )
    sums = down_bins(jnp.transpose(acts, (1, 2, 0)), out_grad, down_index, gate_part, up_part, shares)
    down_sum, gate_sum, up_sum, input_grad = finish(*sums, order, 1.0 / (tokens * ENTRIES))
    return input_grad, gate_sum, up_sum, down_sum


def solution(mesh):
    in_specs = (
        P(None, "inp"),
        P(None, "inp"),
        P("inp", "hid"),
        P("inp", "hid"),
        P("hid", "inp"),
        P(None, "hid"),
        P(None, "hid"),
        P(None, "inp"),
    )
    out_specs = (P("hid", "inp"), P(None, "hid"), P(None, "hid"), P(None, "inp"))
    return jax.shard_map(shards, mesh=mesh, in_specs=in_specs, out_specs=out_specs, check_vma=False)
```
